256 devices in a mesh: seg: 16 (over z, core), sec: 16 (over y, x).
Axes of the slice: x: 4, y: 4, z: 8, core: 2. Of those that a mesh axis runs over, the one named last changes fastest.
Arguments:
- psi: float32 [16, 32, 256, 256], P('seg', 'sec'), may hold values from -6 to 6
- left_env: bfloat16 [16, 6, 32, 256, 256], P('seg', None, 'sec'), may hold values from -1 to 2, as said below
- right_env: bfloat16 [16, 6, 32, 256, 256], P('seg', None, 'sec'), may hold values from -1 to 2, as said below
- hop_outer: bfloat16 [16, 2, 32, 256, 256], P('seg', None, 'sec'), may hold values from -0.75 to 0.75
- hop_inner: bfloat16 [16, 2, 32, 256, 256], P('seg', None, 'sec'), may hold values from -0.75 to 0.75
- dims: int32 [16, 32], P('seg'), may hold values from 1 to 256, 6144 in all within a row
Outputs:
- solution: float32 [16, 32, 256, 256], P('seg', 'sec')
- energy: float32 [16], P('seg')
- env_next: bfloat16 [16, 6, 32, 256, 256], P('seg', None, 'sec')
The draws below stay inside these ranges and needn't reach their ends.
Inputs may be any that keep to these rules, and one draw needn't show every extreme that they name: `left_env`: each block is mostly its diagonal, positive, with small off-diagonal entries. `right_env`: drawn in the same way as left_env. In each segment the dims sum to 6144, and one sector has 256.
All inputs are finite; a program needn't handle non-finite values.
Results may differ from the reference program's by a relative error of at most 0.0085.
Values may be sent and summed in bfloat16 or wider, within the bound.
No kernel may reach another device: no remote copies, remote signals or barrier semaphores. Data moves between devices by JAX's collectives and lax.ppermute only.
A program may use at most 64 MiB of HBM per device.

```python
import math
import jax
import jax.numpy as jnp
import numpy as np
from jax import lax

CAP = 256
NSECT = 32
W = 6
ITERS = 4
LIVE = 6144
NSEG = 16


def env_draw(key, salt):
    shape = (NSEG, W, NSECT, CAP, CAP)
    noise_key, diag_key = jax.random.split(jax.random.fold_in(key, salt))
    noise = jnp.clip(jax.random.normal(noise_key, shape, jnp.float32) * 0.04, -0.16, 0.16)
    diagonal = jnp.exp(jax.random.uniform(diag_key, shape[:-1], jnp.float32, -0.3567, 0.3365))
    indices = jnp.arange(CAP, dtype=jnp.int32)
    identity = (indices[:, None] == indices[None, :]).astype(jnp.float32)
    return noise + identity * diagonal[..., None]


def draw_left_env(key, part):
    return env_draw(key, 17).astype(jnp.bfloat16)


def draw_right_env(key, part):
    return env_draw(key, 29).astype(jnp.bfloat16)


def block_scale(key, shape, pieces, smallest, largest):
    def one(axis_at, shards_of):
        heights = jax.random.uniform(jax.random.fold_in(jax.random.fold_in(key, 6), axis_at), (shards_of,), jnp.float32, smallest / len(pieces), largest / len(pieces))
        return jnp.repeat(jnp.exp(heights), shape[axis_at] // shards_of).reshape((-1,) + (1,) * (len(shape) - axis_at - 1))

    loudness = one(*pieces[0])
    for cut in pieces[1:]:
        loudness = loudness * one(*cut)
    return loudness


def profile(amount, total, most, skew):
    loads = [(1 << 20) // math.isqrt(rank ** skew) + 1 for rank in range(2, amount + 1)]
    surplus, given = total - most - (amount - 1), [1] * (amount - 1)
    while surplus > 0:
        movable = [i for i in range(amount - 1) if given[i] < most]
        mass, left = sum([loads[i] for i in movable]), surplus
        for i in movable:
            addition = min(most - given[i], max(1, left * loads[i] // mass), surplus)
            given[i] = given[i] + addition
            surplus = surplus - addition
    return np.array([most] + given)


def uneven_parts(own_key, number_of, total, limit, slope):
    if number_of == 2:
        one = jax.random.randint(own_key, (), max(1, total - limit), min(limit, total - 1) + 1)
        return jnp.stack([one, total - one])
    sizes = jnp.asarray(profile(number_of, total, limit, slope), jnp.int32)
    pairs = (number_of - 1) // 2
    donor, sink = sizes[1:1 + 2 * pairs:2], sizes[2:2 + 2 * pairs:2]
    margin = jnp.minimum(donor - 1, limit - sink)
    shifted = jax.random.randint(jax.random.fold_in(own_key, 1), (pairs,), 0, 1 << 20) % (margin + 1)
    sizes = sizes.at[1:1 + 2 * pairs:2].set(donor - shifted).at[2:2 + 2 * pairs:2].set(sink + shifted)
    return sizes[jax.random.permutation(jax.random.fold_in(own_key, 2), number_of)]


def bell_draw(rng, shape, width, bound, shards=(), kind=jnp.bfloat16):
    array = jax.random.normal(rng, shape, jnp.float32) * width
    if len(shards) > 0:
        array = block_scale(rng, shape, shards, -0.22, 0.18) * array
    return jnp.clip(array, min=-bound, max=bound).astype(kind)


def setup_inputs(seed: int = 0) -> dict:
    key_of = jax.random.split(jax.random.key(seed), 7)
    psi = bell_draw(key_of[0], (NSEG, NSECT, CAP, CAP), 1.0, 6.0, ((0, 16), (1, 16)), jnp.float32)
    left_env = draw_left_env(jax.random.fold_in(key_of[6], 71), 0)
    right_env = draw_right_env(jax.random.fold_in(key_of[6], 71), 0)
    hop_outer = bell_draw(key_of[3], (NSEG, 2, NSECT, CAP, CAP), (CAP // 4) ** -0.5, 0.75, ((0, 16), (2, 16)))
    hop_inner = bell_draw(key_of[4], (NSEG, 2, NSECT, CAP, CAP), (CAP // 4) ** -0.5, 0.75, ((0, 16), (2, 16)))
    dims = jax.vmap(lambda own: uneven_parts(own, NSECT, LIVE, CAP, 1))(jax.random.split(key_of[5], NSEG)).reshape((NSEG, NSECT)).astype(jnp.int32)
    return {"psi": psi, "left_env": left_env, "right_env": right_env, "hop_outer": hop_outer, "hop_inner": hop_inner, "dims": dims}


TAU = 0.05

def to_half(values):
    rounded = lax.optimization_barrier(values.astype(jnp.bfloat16))
    return rounded.astype(jnp.float32)

def apply_operator(iterate, env_left, env_right, hop_out, hop_in, block_mask):
    rounded = to_half(iterate)
    halfway = to_half(jnp.einsum('sij,wskj->wsik', rounded, env_right.astype(jnp.float32)))
    image = jnp.einsum('wsik,wskj->sij', env_left.astype(jnp.float32), halfway)
    zero_block = jnp.zeros_like(rounded[:1])
    below = jnp.concatenate([zero_block, rounded[:-1]], axis=0)
    above = jnp.concatenate([rounded[1:], zero_block], axis=0)
    hop_out32 = hop_out.astype(jnp.float32)
    hop_in32 = hop_in.astype(jnp.float32)
    lower = to_half(jnp.einsum('sij,skj->sik', below, hop_in32[0]))
    upper = to_half(jnp.einsum('sij,skj->sik', above, hop_in32[1]))
    image = image + jnp.einsum('sik,skj->sij', hop_out32[0], lower)
    image = image + jnp.einsum('sik,skj->sij', hop_out32[1], upper)
    return image * block_mask

def relax(iterate, env_left, env_right, hop_out, hop_in, block_mask, live_count):
    energy = jnp.float32(0.0)
    for sweep_iter in range(ITERS):
        image = apply_operator(iterate, env_left, env_right, hop_out, hop_in, block_mask)
        self_dot = jnp.sum(iterate * iterate)
        cross_dot = jnp.sum(iterate * image)
        energy = cross_dot / self_dot
        step = iterate - TAU * (image - energy * iterate)
        step_norm = jnp.sum(step * step)
        iterate = step * jnp.sqrt(live_count / step_norm)
    return (iterate, energy)

def masks(sector_dims):
    indices = jnp.arange(CAP, dtype=jnp.int32)
    active = (indices[None, :] < sector_dims[:, None]).astype(jnp.float32)
    sizes_f = sector_dims.astype(jnp.float32)
    return (active[:, :, None] * active[:, None, :], jnp.sum(sizes_f * sizes_f))

def first_step(inputs):
    start_psi, env_left, env_right, hop_out, hop_in, sector_dims = inputs
    block_mask, live_count = masks(sector_dims)
    iterate, energy = relax(start_psi * block_mask, env_left, env_right, hop_out, hop_in, block_mask, live_count)
    factor = iterate.astype(jnp.bfloat16).astype(jnp.float32)
    grown = to_half(jnp.einsum('wsik,skj->wsij', env_left.astype(jnp.float32), factor))
    renewed = jnp.einsum('ski,wskj->wsij', factor, grown) / sector_dims.astype(jnp.float32)[None, :, None, None]
    return (iterate, renewed.astype(jnp.bfloat16))

def second_step(inputs):
    iterate, env_left, env_right, hop_out, hop_in, sector_dims = inputs
    block_mask, live_count = masks(sector_dims)
    return relax(iterate, env_left, env_right, hop_out, hop_in, block_mask, live_count)

def reference(psi, left_env, right_env, hop_outer, hop_inner, dims):
    first_iter, env_next = lax.map(first_step, (psi, left_env, right_env, hop_outer, hop_inner, dims))
    boundary = jnp.concatenate([left_env[:1], env_next[:-1]], axis=0)
    solution, energy = lax.map(second_step, (first_iter, boundary, right_env, hop_outer, hop_inner, dims))
    return (solution, energy, env_next)
```

```python
import jax
import jax.numpy as jnp
from jax import lax
from jax.sharding import PartitionSpec as P

ITERS = 4


TAU = 0.05


def passed_along(shard, axis, by):
    length = lax.axis_size(axis)
    pairs = [(i, i + by) for i in range(length) if 0 <= i + by < length]
    return lax.ppermute(shard, axis, pairs)


def row_sum(values, axis):
    size = lax.axis_size(axis)
    rows = jnp.broadcast_to(values[None, None, :], (size, 1, values.shape[0]))
    return jnp.sum(lax.all_to_all(rows, axis, 0, 0), axis=(0, 1))


def apply_operator(iterate, env_left, env_right, hop_out, hop_in, block_mask):
    rounded = iterate.astype(jnp.bfloat16)
    before = passed_along(rounded[-1:], "sec", 1)
    after = passed_along(rounded[:1], "sec", -1)
    padded = jnp.concatenate([before, rounded, after], axis=0)
    halfway = jnp.einsum(
        "sij,wskj->wsik", rounded, env_right, preferred_element_type=jnp.float32
    ).astype(jnp.bfloat16)
    image = jnp.einsum("wsik,wskj->sij", env_left, halfway, preferred_element_type=jnp.float32)
    lower = jnp.einsum(
        "sij,skj->sik", padded[:-2], hop_in[0], preferred_element_type=jnp.float32
    ).astype(jnp.bfloat16)
    upper = jnp.einsum(
        "sij,skj->sik", padded[2:], hop_in[1], preferred_element_type=jnp.float32
    ).astype(jnp.bfloat16)
    image = image + jnp.einsum(
        "sik,skj->sij", hop_out[0], lower, preferred_element_type=jnp.float32
    )
    image = image + jnp.einsum(
        "sik,skj->sij", hop_out[1], upper, preferred_element_type=jnp.float32
    )
    return image * block_mask


def combination(gram, shift, live_count):
    def inner(left, right):
        total = jnp.float32(0.0)
        for i, a in enumerate(left):
            for j, b in enumerate(right):
                if a is not None and b is not None:
                    total = total + a * b * gram[min(i, j), max(i, j)]
        return total

    coefs = [jnp.float32(1.0)]
    energy = jnp.float32(0.0)
    for sweep_iter in range(ITERS):
        raised = [None] + coefs
        offset = (1.0 - inner(coefs, raised) / inner(coefs, coefs)) / TAU
        energy = shift + offset
        moved = [
            (raised[i] if raised[i] is not None else 0.0)
            + (TAU * offset * coefs[i] if i < len(coefs) else 0.0)
            for i in range(len(raised))
        ]
        scale = jnp.sqrt(live_count / inner(moved, moved))
        coefs = [scale * c for c in moved]
    return coefs, energy


def relax(iterate, env_left, env_right, hop_out, hop_in, block_mask, live_count):
    shift = float(env_left.shape[0])
    basis = [iterate]
    for sweep_iter in range(ITERS):
        image = apply_operator(basis[-1], env_left, env_right, hop_out, hop_in, block_mask)
        basis.append(basis[-1] - TAU * (image - shift * basis[-1]))
    pairs = [(i, j) for i in range(ITERS + 1) for j in range(i, ITERS + 1)]
    dots = jnp.stack([jnp.sum(basis[i] * basis[j]) for i, j in pairs])
    dots = row_sum(jnp.pad(dots, (0, 128 - len(pairs))), "sec")
    gram = {pair: dots[n] for n, pair in enumerate(pairs)}
    coefs, energy = combination(gram, shift, live_count)
    return (sum(c * v for c, v in zip(coefs, basis)), energy)


def grow(env_left, factor, own_dims):
    grown = jnp.einsum(
        "wsik,skj->wsij", env_left, factor, preferred_element_type=jnp.float32
    ).astype(jnp.bfloat16)
    renewed = jnp.einsum("ski,wskj->wsij", factor, grown, preferred_element_type=jnp.float32)
    return (renewed / own_dims.astype(jnp.float32)[None, :, None, None]).astype(jnp.bfloat16)


def body(psi, left_env, right_env, hop_outer, hop_inner, dims):
    sectors_here = psi.shape[1]
    capacity = psi.shape[2]
    first_sector = lax.axis_index("sec") * sectors_here
    env_left = left_env[0]
    env_right = right_env[0]
    hop_out = hop_outer[0]
    hop_in = hop_inner[0]
    earlier_env = passed_along(env_left, "seg", 1)
    earlier_dims = passed_along(dims[0], "seg", 1)
    own_dims = lax.dynamic_slice_in_dim(dims[0], first_sector, sectors_here)
    earlier_dims = lax.dynamic_slice_in_dim(earlier_dims, first_sector, sectors_here)
    sizes_f = dims[0].astype(jnp.float32)
    live_count = jnp.sum(sizes_f * sizes_f)
    indices = jnp.arange(capacity, dtype=jnp.int32)
    active = (indices[None, :] < own_dims[:, None]).astype(jnp.float32)
    block_mask = active[:, :, None] * active[:, None, :]
    iterate, energy = relax(
        psi[0] * block_mask, env_left, env_right, hop_out, hop_in, block_mask, live_count
    )
    factor = iterate.astype(jnp.bfloat16)
    earlier_factor = passed_along(factor, "seg", 1)
    renewed = grow(env_left, factor, own_dims)
    boundary = jnp.where(
        lax.axis_index("seg") == 0,
        env_left,
        grow(earlier_env, earlier_factor, jnp.maximum(earlier_dims, 1)),
    )
    iterate, energy = relax(iterate, boundary, env_right, hop_out, hop_in, block_mask, live_count)
    return (iterate[None], jnp.reshape(energy, (1,)), renewed[None])


def solution(mesh):
    return jax.shard_map(
        body,
        mesh=mesh,
        in_specs=(
            P("seg", "sec", None, None),
            P("seg", None, "sec", None, None),
            P("seg", None, "sec", None, None),
            P("seg", None, "sec", None, None),
            P("seg", None, "sec", None, None),
            P("seg", None),
        ),
        out_specs=(P("seg", "sec", None, None), P("seg"), P("seg", None, "sec", None, None)),
        check_vma=False,
    )
```

```python
import functools

import jax
import jax.numpy as jnp
from jax import lax
from jax.experimental import pallas as pl
from jax.experimental.pallas import tpu as pltpu
from jax.sharding import PartitionSpec as P

ITERS = 4
TAU = 0.05
F32 = jnp.float32
BF16 = jnp.bfloat16
LANES = 128
VMEM_LIMIT = 24 << 20
ROWS = 8

VMEM = pl.BlockSpec(memory_space=pltpu.VMEM)
SMEM = pl.BlockSpec(memory_space=pltpu.SMEM)


def nn(a, b):
    return lax.dot_general(a, b, (((1,), (0,)), ((), ())), preferred_element_type=F32)


def nt(a, b):
    return lax.dot_general(a, b, (((1,), (1,)), ((), ())), preferred_element_type=F32)


def hop(block, inner, outer):
    return nn(outer, nt(block, inner).astype(BF16))


def active(dim, cap):
    rows = lax.broadcasted_iota(jnp.int32, (cap, cap), 0)
    cols = lax.broadcasted_iota(jnp.int32, (cap, cap), 1)
    return jnp.logical_and(rows < dim, cols < dim)


def masked(block, dim):
    return jnp.where(active(dim, block.shape[-1]), block, 0.0)


def local_part(v, env, right, outer, inner, dims, first, shift):
    held = len(v)
    b = [x.astype(BF16) for x in v]
    out = []
    for s in range(held):
        image = None
        for w in range(right.shape[1]):
            term = nn(env(w, s), nt(b[s], right[0, w, s]).astype(BF16))
            image = term if image is None else image + term
        if s > 0:
            image = image + hop(b[s - 1], inner[0, 0, s], outer[0, 0, s])
        if s + 1 < held:
            image = image + hop(b[s + 1], inner[0, 1, s], outer[0, 1, s])
        out.append(v[s] - TAU * (masked(image, dims[0, first + s]) - shift * v[s]))
    return out


def dot_rows(basis, last):
    rows = lax.broadcasted_iota(jnp.int32, (ROWS, LANES), 0)
    out = jnp.zeros((ROWS, LANES), F32)
    for i, other in enumerate(basis):
        total = sum(jnp.sum(a * b, axis=0, keepdims=True) for a, b in zip(other, last))
        total = sum(total[:, n : n + LANES] for n in range(0, total.shape[1], LANES))
        out = jnp.where(rows == i, total, out)
    return out


def put_edges(odd, low, high, inside, across):
    inside[...] = jnp.where(odd, low, high)
    across[...] = jnp.where(odd, high, low)


def edges_from(odd, inside, across):
    return jnp.where(odd, inside, across), jnp.where(odd, across, inside)


def is_odd(place):
    return place[0] % 2 == 1


def start_kernel(
    place, dims, psi, low_outer, low_inner, high_outer, high_inner, v0, inside, across
):
    held = psi.shape[1]
    first = place[0] * held
    odd = is_odd(place)
    blocks = [masked(psi[0, s], dims[0, first + s]) for s in range(held)]
    for s in range(held):
        v0[s] = blocks[s]
    low = [blocks[0].astype(BF16), low_outer[0, 0, 0], low_inner[0, 0, 0]]
    high = [blocks[-1].astype(BF16), high_outer[0, 0, 0], high_inner[0, 0, 0]]
    for n in range(3):
        inside[n] = jnp.where(odd, low[n], high[n])
        across[n] = jnp.where(odd, high[n], low[n])


def local_kernel(shift, place, dims, v0, left, right, outer, inner, q, inside, across, dots):
    held = v0.shape[0]
    v = [v0[s] for s in range(held)]
    out = local_part(
        v, lambda w, s: left[0, w, s], right, outer, inner, dims, place[0] * held, shift
    )
    for s in range(held):
        q[s] = out[s]
    put_edges(is_odd(place), out[0].astype(BF16), out[-1].astype(BF16), inside, across)
    dots[...] = dot_rows([v], v)


def ghosts(k, place, dims, v_before, inside, across, hops_inside, hops_across):
    odd = is_odd(place)
    if k == 0:
        return edges_from(odd, inside[0], across[0])
    low, high = edges_from(odd, inside[...], across[...])
    held = v_before.shape[0]
    first = place[0] * held
    last = dims.shape[1] - 1
    low_dim = dims[0, jnp.maximum(first - 1, 0)]
    high_dim = dims[0, jnp.minimum(first + held, last)]
    low_outer, high_outer = edges_from(odd, hops_inside[1], hops_across[1])
    low_inner, high_inner = edges_from(odd, hops_inside[2], hops_across[2])
    into_low = hop(v_before[0].astype(BF16), low_inner, low_outer)
    into_high = hop(v_before[held - 1].astype(BF16), high_inner, high_outer)
    low = (low.astype(F32) - TAU * masked(into_low, low_dim)).astype(BF16)
    high = (high.astype(F32) - TAU * masked(into_high, high_dim)).astype(BF16)
    return low, high


def step_kernel(k, keep, shift, names, *refs):
    r = dict(zip(names, refs))
    place, dims, q, outer, inner = (r[n] for n in ("place", "dims", "q", "outer", "inner"))
    held = q.shape[0]
    first = place[0] * held
    if "came_inside" in r:
        low, high = ghosts(
            k,
            place,
            dims,
            r.get("v_before"),
            r["came_inside"],
            r["came_across"],
            r.get("hops_inside"),
            r.get("hops_across"),
        )
    else:
        low, high = r["at_low"][...], r["at_high"][...]
    if keep:
        r["ghost_low"][...] = low
        r["ghost_high"][...] = high
    v = [q[s] for s in range(held)]
    v[0] = v[0] - TAU * masked(hop(low, inner[0, 0, 0], outer[0, 0, 0]), dims[0, first])
    v[-1] = v[-1] - TAU * masked(
        hop(high, inner[0, 1, held - 1], outer[0, 1, held - 1]), dims[0, first + held - 1]
    )
    for s in range(held):
        r["v"][s] = v[s]
    basis = [[r[f"v{i}"][s] for s in range(held)] for i in range(k + 1)]
    if k + 1 < ITERS:
        left = r["left"]
        env = (lambda w, s: left[0, w, s]) if len(left.shape) == 5 else (lambda w, s: left[w, s])
        out = local_part(v, env, r["right"], outer, inner, dims, first, shift)
        for s in range(held):
            r["q_next"][s] = out[s]
        put_edges(
            is_odd(place), out[0].astype(BF16), out[-1].astype(BF16), r["inside"], r["across"]
        )
        r["dots"][...] = dot_rows(basis + [v], v)
    else:
        lanes = lax.broadcasted_iota(jnp.int32, (ROWS, LANES), 1)
        rows = lax.broadcasted_iota(jnp.int32, (ROWS, LANES), 0)
        line = jnp.zeros((1, LANES), F32)
        for j in range(ITERS + 1):
            part = r[f"dots{j}"][...] if j < ITERS else dot_rows(basis + [v], v)
            part = jnp.sum(part, axis=1, keepdims=True)
            line = line + jnp.sum(
                jnp.where(lanes == ROWS * j + rows, part, 0.0), axis=0, keepdims=True
            )
        for n in range(r["line"].shape[0]):
            r["line"][n] = line


def combination(line, live_count, shift):
    lanes = lax.broadcasted_iota(jnp.int32, (1, LANES), 1)
    gram = {}
    for j in range(ITERS + 1):
        for i in range(j + 1):
            gram[i, j] = jnp.sum(
                jnp.where(lanes == ROWS * j + i, line, 0.0), axis=1, keepdims=True
            )
            gram[j, i] = gram[i, j]
    coefs = [jnp.ones((1, 1), F32)]
    energy = None
    for _ in range(ITERS):
        n = len(coefs)
        onto = [sum(coefs[i] * gram[i, j] for i in range(n)) for j in range(n + 1)]
        raised = [sum(coefs[i] * gram[i + 1, j] for i in range(n)) for j in range(1, n + 1)]
        self_dot = sum(coefs[j] * onto[j] for j in range(n))
        cross = sum(coefs[j] * onto[j + 1] for j in range(n))
        square = sum(coefs[j] * raised[j] for j in range(n))
        ratio = cross / self_dot
        gain = 1.0 - ratio
        energy = shift + gain / TAU
        norm = square + gain * (2.0 * cross + gain * self_dot)
        scale = jnp.sqrt(live_count / norm)
        moved = [gain * c for c in coefs] + [jnp.zeros((1, 1), F32)]
        moved = [moved[0]] + [moved[i + 1] + coefs[i] for i in range(n)]
        coefs = [scale * c for c in moved]
    return coefs, energy


def live_count_of(dims):
    total = jnp.int32(0)
    for s in range(dims.shape[1]):
        total = total + dims[0, s] * dims[0, s]
    return jnp.full((1, 1), total.astype(F32))


def join_kernel(shift, names, *refs):
    r = dict(zip(names, refs))
    place, dims = r["place"], r["dims"]
    line = jnp.sum(r["lines"][...], axis=0)
    coefs, _ = combination(line, live_count_of(dims), shift)
    held, cap, _ = r["v0"].shape
    for s in range(held):
        block = sum(c * r[f"v{k}"][s] for k, c in enumerate(coefs))
        r["x"][s] = block
        r["factor"][s, :cap] = block.astype(BF16)
        r["factor"][s, cap:] = jnp.full(
            (r["factor"].shape[1] - cap, cap), dims[0, place[0] * held + s].astype(F32)
        ).astype(BF16)
    low, high = ghosts(
        ITERS,
        place,
        dims,
        r[f"v{ITERS - 1}"],
        r["came_inside"],
        r["came_across"],
        r["hops_inside"],
        r["hops_across"],
    )
    for side, last in (("low", low), ("high", high)):
        blocks = [r[f"ghost_{side}{k}"][...] for k in range(ITERS)] + [last]
        total = sum(c * b.astype(F32) for c, b in zip(coefs, blocks))
        r[f"at_{side}"][...] = total.astype(BF16)


def grow_kernel(left, factor, out):
    held, cap = left.shape[2], left.shape[3]
    for s in range(held):
        block = factor[s, :cap]
        dim = factor[s, cap : cap + 1].astype(F32)
        for w in range(left.shape[1]):
            product = nn(block.T, nn(left[0, w, s], block).astype(BF16))
            out[0, w, s] = (product / dim).astype(BF16)


def second_kernel(
    shift, place, dims, x, left, earlier, factor, right, outer, inner, env, q, inside, across, dots
):
    held, cap, _ = x.shape

    @pl.when(place[1] == 0)
    def _():
        env[...] = left[0]

    @pl.when(place[1] != 0)
    def _():
        for s in range(held):
            block = factor[s, :cap]
            dim = factor[s, cap : cap + 1].astype(F32)
            for w in range(left.shape[1]):
                product = nn(block.T, nn(earlier[0, w, s], block).astype(BF16))
                env[w, s] = (product / dim).astype(BF16)

    v = [x[s] for s in range(held)]
    out = local_part(v, lambda w, s: env[w, s], right, outer, inner, dims, place[0] * held, shift)
    for s in range(held):
        q[s] = out[s]
    put_edges(is_odd(place), out[0].astype(BF16), out[-1].astype(BF16), inside, across)
    dots[...] = dot_rows([v], v)


def finish_kernel(shift, names, *refs):
    r = dict(zip(names, refs))
    line = jnp.sum(r["lines"][...], axis=0)
    coefs, energy = combination(line, live_count_of(r["dims"]), shift)
    for s in range(r["v0"].shape[0]):
        r["x"][0, s] = sum(c * r[f"v{k}"][s] for k, c in enumerate(coefs))
    r["energy"][0] = energy[0, 0]


def struct(shape, dtype):
    return jax.ShapeDtypeStruct(shape, dtype)


def call(kernel, name, outs, *args, flops=0, specs=None, grid=()):
    return pl.pallas_call(
        kernel,
        out_shape=tuple(outs),
        grid=grid,
        in_specs=specs or [SMEM if a.dtype == jnp.int32 else VMEM for a in args],
        out_specs=tuple(SMEM if o.shape == (1,) else VMEM for o in outs),
        name=name,
        compiler_params=pltpu.CompilerParams(vmem_limit_bytes=VMEM_LIMIT),
        cost_estimate=pl.CostEstimate(
            flops=flops,
            transcendentals=0,
            bytes_accessed=sum(a.size * a.dtype.itemsize for a in args),
        ),
    )(*args)


def named(kernel, name, ins, outs, flops=0):
    values = call(
        functools.partial(kernel, tuple(ins) + tuple(outs)),
        name,
        outs.values(),
        *ins.values(),
        flops=flops,
    )
    return dict(zip(outs, values))


def body(psi, left_env, right_env, hop_outer, hop_inner, dims):
    _, terms, held, cap, _ = left_env.shape
    shift = float(terms)
    size = lax.axis_size("sec")
    place = jnp.stack([lax.axis_index("sec"), lax.axis_index("seg")]).astype(jnp.int32)
    block = struct((cap, cap), BF16)
    blocks = struct((held, cap, cap), F32)
    triple = struct((3, cap, cap), BF16)
    dots_of = struct((ROWS, LANES), F32)
    pairs = [(i, i ^ 1) for i in range(size)]
    others = [(i, i + 1 if i % 2 else i - 1) for i in range(1, size - 1)]
    onward = [(i, i + 1) for i in range(lax.axis_size("seg") - 1)]
    one = 2 * cap**3

    def exchange(inside, across):
        return lax.ppermute(inside, "sec", pairs), lax.ppermute(across, "sec", others)

    def relaxed(v0, q, sent, first, dots, env, hops, keep):
        basis = {"v0": v0}
        all_dots = {"dots0": dots}
        kept = {}
        before = first
        for k in range(ITERS):
            came = exchange(*sent)
            ins = {"place": place, "dims": dims, "q": q, "outer": hop_outer, "inner": hop_inner}
            ins.update(basis)
            ins.update(before)
            if k > 0:
                ins.update(v_before=basis[f"v{k - 1}"], hops_inside=hops[0], hops_across=hops[1])
            outs = {"v": blocks}
            if keep:
                outs.update(ghost_low=block, ghost_high=block)
            if k + 1 < ITERS:
                ins.update(left=env, right=right_env)
                outs.update(q_next=blocks, inside=block, across=block, dots=dots_of)
            else:
                ins.update(all_dots)
                outs.update(line=struct((size, 1, LANES), F32))
            got = named(
                functools.partial(step_kernel, k, keep, shift),
                f"step{k}",
                ins,
                outs,
                flops=one * 36,
            )
            basis[f"v{k + 1}"] = got["v"]
            if keep:
                kept[f"ghost_low{k}"], kept[f"ghost_high{k}"] = got["ghost_low"], got["ghost_high"]
            before = {"came_inside": came[0], "came_across": came[1]}
            if k + 1 < ITERS:
                q, sent = got["q_next"], (got["inside"], got["across"])
                all_dots[f"dots{k + 1}"] = got["dots"]
        lines = lax.all_to_all(got["line"], "sec", 0, 0)
        return basis, kept, lines, before

    def block_at(side, sector):
        return pl.BlockSpec((1, 1, 1, cap, cap), lambda n: (0, side, sector, 0, 0))

    v0, inside, across = call(
        start_kernel,
        "start",
        (blocks, triple, triple),
        place,
        dims,
        psi,
        hop_outer,
        hop_inner,
        hop_outer,
        hop_inner,
        specs=[SMEM, SMEM, VMEM] + 2 * [block_at(0, 0)] + 2 * [block_at(1, held - 1)],
        grid=(1,),
    )
    hops = exchange(inside, across)
    earlier = lax.ppermute(left_env, "seg", onward)
    q, inside, across, dots = call(
        functools.partial(local_kernel, shift),
        "local",
        (blocks, block, block, dots_of),
        place,
        dims,
        v0,
        left_env,
        right_env,
        hop_outer,
        hop_inner,
        flops=one * 28,
    )
    first = {"came_inside": hops[0], "came_across": hops[1]}
    basis, kept, lines, last = relaxed(
        v0, q, (inside, across), first, dots, left_env, hops, True
    )
    ins = {"place": place, "dims": dims, "lines": lines}
    ins.update(basis)
    ins.update(kept)
    ins.update(last)
    ins.update(hops_inside=hops[0], hops_across=hops[1])
    outs = {
        "x": blocks,
        "factor": struct((held, cap + 16, cap), BF16),
        "at_low": block,
        "at_high": block,
    }
    got = named(functools.partial(join_kernel, shift), "join", ins, outs, flops=one * 4)
    x, factor = got["x"], got["factor"]
    earlier_factor = lax.ppermute(factor, "seg", onward)
    (renewed,) = call(
        grow_kernel, "grow", (struct(left_env.shape, BF16),), left_env, factor, flops=one * 24
    )
    env, q, inside, across, dots = call(
        functools.partial(second_kernel, shift),
        "second",
        (struct((terms, held, cap, cap), BF16), blocks, block, block, dots_of),
        place,
        dims,
        x,
        left_env,
        earlier,
        earlier_factor,
        right_env,
        hop_outer,
        hop_inner,
        flops=one * 52,
    )
    first = {"at_low": got["at_low"], "at_high": got["at_high"]}
    basis, _, lines, _ = relaxed(x, q, (inside, across), first, dots, env, hops, False)
    ins = {"dims": dims, "lines": lines}
    ins.update(basis)
    outs = {"x": struct(psi.shape, F32), "energy": struct((1,), F32)}
    got = named(functools.partial(finish_kernel, shift), "finish", ins, outs)
    return (got["x"], got["energy"], renewed)


def solution(mesh):
    return jax.shard_map(
        body,
        mesh=mesh,
        in_specs=(
            P("seg", "sec", None, None),
            P("seg", None, "sec", None, None),
            P("seg", None, "sec", None, None),
            P("seg", None, "sec", None, None),
            P("seg", None, "sec", None, None),
            P("seg", None),
        ),
        out_specs=(P("seg", "sec", None, None), P("seg"), P("seg", None, "sec", None, None)),
        check_vma=False,
    )
```

```python
import functools

import jax
import jax.numpy as jnp
from jax import lax
from jax.experimental import pallas as pl
from jax.experimental.pallas import tpu as pltpu
from jax.sharding import PartitionSpec as P

ITERS = 4
TAU = 0.05
F32 = jnp.float32
BF16 = jnp.bfloat16
LANES = 128
VMEM_LIMIT = 24 << 20
ROWS = 8

VMEM = pl.BlockSpec(memory_space=pltpu.VMEM)
SMEM = pl.BlockSpec(memory_space=pltpu.SMEM)
HBM = pl.BlockSpec(memory_space=pltpu.HBM)


def nn(a, b):
    return lax.dot_general(a, b, (((1,), (0,)), ((), ())), preferred_element_type=F32)


def nt(a, b):
    return lax.dot_general(a, b, (((1,), (1,)), ((), ())), preferred_element_type=F32)


def hop(block, inner, outer):
    return nn(outer, nt(block, inner).astype(BF16))


def masked(block, dim):
    rows = lax.broadcasted_iota(jnp.int32, block.shape, 0)
    cols = lax.broadcasted_iota(jnp.int32, block.shape, 1)
    return jnp.where(jnp.logical_and(rows < dim, cols < dim), block, 0.0)


def local_part(v, env, right, outer, inner, shift):
    held = len(v)
    terms = right.shape[1]
    b = [x.astype(BF16) for x in v]
    half = [[nt(b[s], right[0, w, s]).astype(BF16) for s in range(held)] for w in range(terms)]
    image = [None] * held
    for s in range(held):
        if s > 0:
            image[s] = hop(b[s - 1], inner[0, 0, s], outer[0, 0, s])
        if s + 1 < held:
            above = hop(b[s + 1], inner[0, 1, s], outer[0, 1, s])
            image[s] = above if image[s] is None else image[s] + above
    for w in range(terms):
        for s in range(held):
            term = nn(env(w, s), half[w][s])
            image[s] = term if image[s] is None else image[s] + term
    return [v[s] * (1.0 + TAU * shift) - TAU * image[s] for s in range(held)]


def dot_rows(basis, last):
    rows = lax.broadcasted_iota(jnp.int32, (ROWS, LANES), 0)
    out = jnp.zeros((ROWS, LANES), F32)
    for i, other in enumerate(basis):
        total = sum(jnp.sum(a * b, axis=0, keepdims=True) for a, b in zip(other, last))
        total = sum(total[:, n : n + LANES] for n in range(0, total.shape[1], LANES))
        out = jnp.where(rows == i, total, out)
    return out


class Facts:
    ODD, FIRST, LIVE, INSIDE, ACROSS, DIM = range(6)

    def __init__(self, ref):
        self.ref = ref

    def row(self, n):
        return self.ref[n : n + 1, 0:1]

    @property
    def odd(self):
        return self.row(self.ODD) == 1

    def dim(self, s):
        return self.row(self.DIM + s)


def swapped(odd, low, high):
    return jnp.where(odd, low, high), jnp.where(odd, high, low)


def start_kernel(
    place, dims, psi_at, outer_at, inner_at, v0, inside, across, facts, psi, blocks, arrived
):
    held, cap, _ = psi.shape
    copies = [pltpu.make_async_copy(psi_at.at[0, s], psi.at[s], arrived.at[s]) for s in range(held)]
    for n, (side, s) in enumerate(((0, 0), (1, held - 1))):
        for m, array in enumerate((outer_at, inner_at)):
            copies.append(
                pltpu.make_async_copy(
                    array.at[0, side, s], blocks.at[2 * n + m], arrived.at[held + 2 * n + m]
                )
            )
    for copy in copies:
        copy.start()
    first = place[0] * held
    last = dims.shape[1] - 1
    odd = place[0] % 2
    low_dim = dims[0, jnp.maximum(first - 1, 0)]
    high_dim = dims[0, jnp.minimum(first + held, last)]
    live = jnp.int32(0)
    for s in range(dims.shape[1]):
        live = live + dims[0, s] * dims[0, s]
    rows = [
        odd,
        jnp.where(place[1] == 0, 1, 0),
        live,
        jnp.where(odd == 1, low_dim, high_dim),
        jnp.where(odd == 1, high_dim, low_dim),
    ] + [dims[0, first + s] for s in range(held)]
    for n, value in enumerate(rows):
        facts[n : n + 1, :] = jnp.full((1, LANES), value, jnp.int32)
    for copy in copies[:held]:
        copy.wait()
    edges = [masked(psi[s], dims[0, first + s]) for s in range(held)]
    for s in range(held):
        v0[s] = edges[s]
    low = edges[0].astype(BF16)
    high = edges[-1].astype(BF16)
    inside[0] = jnp.where(odd == 1, low, high)
    across[0] = jnp.where(odd == 1, high, low)
    for copy in copies[held:]:
        copy.wait()
    for m in range(2):
        inside[1 + m] = jnp.where(odd == 1, blocks[m], blocks[2 + m])
        across[1 + m] = jnp.where(odd == 1, blocks[2 + m], blocks[m])


def put_local(v, env, r, shift):
    facts = Facts(r["facts"])
    out = local_part(v, env, r["right"], r["outer"], r["inner"], shift)
    for s, block in enumerate(out):
        r["q"][s] = block
    inside, across = swapped(facts.odd, out[0], out[-1])
    r["inside"][...] = inside.astype(BF16)
    r["across"][...] = across.astype(BF16)


def local_kernel(shift, names, *refs):
    r = dict(zip(names, refs))
    v = [r["v0"][s] for s in range(r["v0"].shape[0])]
    put_local(v, lambda w, s: r["left"][0, w, s], r, shift)
    r["dots"][...] = dot_rows([v], v)


def ghosts(k, facts, r):
    came = [r["came_inside"], r["came_across"]]
    came = [(c[0] if len(c.shape) == 3 else c[...]).astype(F32) for c in came]
    if k > 0:
        before = r[f"v{k - 1}"]
        sent = swapped(facts.odd, before[0], before[before.shape[0] - 1])
        dims = (facts.row(facts.INSIDE), facts.row(facts.ACROSS))
        hops = (r["hops_inside"], r["hops_across"])
        came = [
            masked(c - TAU * hop(b.astype(BF16), h[2], h[1]), d)
            for c, b, h, d in zip(came, sent, hops, dims)
        ]
    low, high = swapped(facts.odd, *came)
    return low.astype(BF16), high.astype(BF16)


def step_kernel(k, shift, names, *refs):
    r = dict(zip(names, refs))
    facts = Facts(r["facts"])
    outer, inner = r["outer"], r["inner"]
    held = r["part"].shape[0]
    low, high = ghosts(k, facts, r)
    v = [r["part"][s] for s in range(held)]
    v[0] = v[0] - TAU * hop(low, inner[0, 0, 0], outer[0, 0, 0])
    v[-1] = v[-1] - TAU * hop(high, inner[0, 1, held - 1], outer[0, 1, held - 1])
    v = [masked(block, facts.dim(s)) for s, block in enumerate(v)]
    for s in range(held):
        r["v"][s] = v[s]
    basis = [[r[f"v{i}"][s] for s in range(held)] for i in range(k + 1)]
    if k + 1 < ITERS:
        left = r["left"]
        env = (lambda w, s: left[0, w, s]) if len(left.shape) == 5 else (lambda w, s: left[w, s])
        put_local(v, env, r, shift)
        r["dots"][...] = dot_rows(basis + [v], v)
    else:
        lanes = lax.broadcasted_iota(jnp.int32, (ROWS, LANES), 1)
        rows = lax.broadcasted_iota(jnp.int32, (ROWS, LANES), 0)
        line = jnp.zeros((1, LANES), F32)
        for j in range(ITERS + 1):
            part = r[f"dots{j}"][...] if j < ITERS else dot_rows(basis + [v], v)
            part = jnp.sum(part, axis=1, keepdims=True)
            line = line + jnp.sum(
                jnp.where(lanes == ROWS * j + rows, part, 0.0), axis=0, keepdims=True
            )
        for n in range(r["line"].shape[0]):
            r["line"][n] = line


def combination(line, live_count, shift):
    lanes = lax.broadcasted_iota(jnp.int32, (1, LANES), 1)
    gram = {}
    for j in range(ITERS + 1):
        for i in range(j + 1):
            gram[i, j] = jnp.sum(
                jnp.where(lanes == ROWS * j + i, line, 0.0), axis=1, keepdims=True
            )
            gram[j, i] = gram[i, j]
    coefs = [jnp.ones((1, 1), F32)]
    energy = None
    for _ in range(ITERS):
        n = len(coefs)
        onto = [sum(coefs[i] * gram[i, j] for i in range(n)) for j in range(n + 1)]
        raised = [sum(coefs[i] * gram[i + 1, j] for i in range(n)) for j in range(1, n + 1)]
        self_dot = sum(coefs[j] * onto[j] for j in range(n))
        cross = sum(coefs[j] * onto[j + 1] for j in range(n))
        square = sum(coefs[j] * raised[j] for j in range(n))
        ratio = cross / self_dot
        gain = 1.0 - ratio
        energy = shift + gain / TAU
        norm = square + gain * (2.0 * cross + gain * self_dot)
        scale = jnp.sqrt(live_count / norm)
        moved = [gain * c for c in coefs] + [jnp.zeros((1, 1), F32)]
        moved = [moved[0]] + [moved[i + 1] + coefs[i] for i in range(n)]
        coefs = [scale * c for c in moved]
    return coefs, energy


def join_kernel(shift, names, *refs):
    r = dict(zip(names, refs))
    facts = Facts(r["facts"])
    line = jnp.sum(r["lines"][...], axis=0)
    coefs, _ = combination(line, facts.row(facts.LIVE).astype(F32), shift)
    held, cap, _ = r["v0"].shape
    pad = r["factor"].shape[1] - cap
    blocks = [sum(c * r[f"v{k}"][s] for k, c in enumerate(coefs)) for s in range(held)]
    for s, block in enumerate(blocks):
        r["x"][s] = block
        r["factor"][s, :cap] = block.astype(BF16)
        dim = jnp.broadcast_to(facts.dim(s).astype(F32), (pad, cap))
        r["factor"][s, cap:] = dim.astype(BF16)
    inside, across = swapped(facts.odd, blocks[0], blocks[-1])
    r["inside"][...] = inside.astype(BF16)
    r["across"][...] = across.astype(BF16)


def grown(env, factor):
    cap = env.shape[0]
    block = factor[:cap]
    product = nn(block.T, nn(env, block).astype(BF16))
    return (product / factor[cap : cap + 1].astype(F32)).astype(BF16)


def grow_kernel(left, factor, out, token):
    for s in range(left.shape[2]):
        for w in range(left.shape[1]):
            out[0, w, s] = grown(left[0, w, s], factor[s])
    token[...] = jnp.zeros_like(token)


def second_kernel(shift, names, *refs):
    r = dict(zip(names, refs))
    facts = Facts(r["facts"])
    held = r["v0"].shape[0]
    first = facts.row(facts.FIRST) == 1
    for s in range(held):
        for w in range(r["left"].shape[1]):
            new = grown(r["earlier"][0, w, s], r["factor"][s]).astype(F32)
            kept = r["left"][0, w, s].astype(F32)
            r["env"][w, s] = jnp.where(first, kept, new).astype(BF16)
    v = [r["v0"][s] for s in range(held)]
    put_local(v, lambda w, s: r["env"][w, s], r, shift)
    r["dots"][...] = dot_rows([v], v)


def finish_kernel(shift, names, *refs):
    r = dict(zip(names, refs))
    facts = Facts(r["facts"])
    line = jnp.sum(r["lines"][...], axis=0)
    coefs, energy = combination(line, facts.row(facts.LIVE).astype(F32), shift)
    for s in range(r["v0"].shape[0]):
        r["x"][0, s] = sum(c * r[f"v{k}"][s] for k, c in enumerate(coefs))
    r["energy"][0] = energy[0, 0]


def struct(shape, dtype):
    return jax.ShapeDtypeStruct(shape, dtype)


def call(kernel, name, ins, outs, flops=0, specs=None, scratch=()):
    args = tuple(ins.values())
    values = pl.pallas_call(
        kernel,
        out_shape=tuple(outs.values()),
        in_specs=specs or [VMEM] * len(args),
        out_specs=tuple(SMEM if o.shape == (1,) else VMEM for o in outs.values()),
        scratch_shapes=scratch,
        name=name,
        compiler_params=pltpu.CompilerParams(vmem_limit_bytes=VMEM_LIMIT),
        cost_estimate=pl.CostEstimate(
            flops=flops,
            transcendentals=0,
            bytes_accessed=sum(a.size * a.dtype.itemsize for a in args),
        ),
    )(*args)
    return dict(zip(outs, values))


def body(psi, left_env, right_env, hop_outer, hop_inner, dims):
    _, terms, held, cap, _ = left_env.shape
    shift = float(terms)
    size = lax.axis_size("sec")
    place = jnp.stack([lax.axis_index("sec"), lax.axis_index("seg")]).astype(jnp.int32)
    block = struct((cap, cap), BF16)
    blocks = struct((held, cap, cap), F32)
    triple = struct((3, cap, cap), BF16)
    dots_of = struct((ROWS, LANES), F32)
    local_outs = {"q": blocks, "inside": block, "across": block, "dots": dots_of}
    pairs = [(i, i ^ 1) for i in range(size)]
    others = [(i, i + 1 if i % 2 else i - 1) for i in range(1, size - 1)]
    onward = [(i, i + 1) for i in range(lax.axis_size("seg") - 1)]
    one = 2 * cap**3

    def exchange(got):
        return {
            "came_inside": lax.ppermute(got["inside"], "sec", pairs),
            "came_across": lax.ppermute(got["across"], "sec", others),
        }

    def made(kernel, name, ins, outs, flops=0):
        names = tuple(ins) + tuple(outs)
        return call(functools.partial(kernel, names), name, ins, outs, flops)

    start = call(
        start_kernel,
        "start",
        {"place": place, "dims": dims, "psi": psi, "outer": hop_outer, "inner": hop_inner},
        {
            "v0": blocks,
            "inside": triple,
            "across": triple,
            "facts": struct((ROWS * (1 + (4 + held) // ROWS), LANES), jnp.int32),
        },
        specs=[SMEM, SMEM, HBM, HBM, HBM],
        scratch=[
            pltpu.VMEM((held, cap, cap), F32),
            pltpu.VMEM((4, cap, cap), BF16),
            pltpu.SemaphoreType.DMA((held + 4,)),
        ],
    )
    facts = start["facts"]
    common = {"facts": facts, "outer": hop_outer, "inner": hop_inner, "right": right_env}
    came = exchange(start)
    hops = {"hops_inside": came["came_inside"], "hops_across": came["came_across"]}
    earlier = lax.ppermute(left_env, "seg", onward)

    def relaxed(v0, came, got, env):
        basis = {"v0": v0}
        dots = {"dots0": got["dots"]}
        for k in range(ITERS):
            ins = {"part": got["q"], **common, **basis, **came}
            if k > 0:
                ins.update(hops)
            if k + 1 < ITERS:
                came = exchange(got)
                ins.update(left=env)
                outs = {"v": blocks, **local_outs}
            else:
                del ins["right"]
                ins.update(dots)
                outs = {"v": blocks, "line": struct((size, 1, LANES), F32)}
            kernel = functools.partial(step_kernel, k, shift)
            got = made(kernel, f"step{k}", ins, outs, flops=one * 36)
            basis[f"v{k + 1}"] = got["v"]
            if k + 1 < ITERS:
                dots[f"dots{k + 1}"] = got["dots"]
        return basis, lax.all_to_all(got["line"], "sec", 0, 0)

    got = made(
        functools.partial(local_kernel, shift),
        "local",
        {"v0": start["v0"], "left": left_env, **common},
        local_outs,
        flops=one * 28,
    )
    basis, lines = relaxed(start["v0"], came, got, left_env)
    joined = made(
        functools.partial(join_kernel, shift),
        "join",
        {"facts": facts, "lines": lines, **basis},
        {
            "x": blocks,
            "factor": struct((held, cap + 16, cap), BF16),
            "inside": block,
            "across": block,
        },
    )
    factor = joined["factor"]
    earlier_factor = lax.ppermute(factor, "seg", onward)
    came = exchange(joined)
    renewed = call(
        grow_kernel,
        "grow",
        {"left": left_env, "factor": factor},
        {"out": struct(left_env.shape, BF16), "token": dots_of},
        flops=one * 24,
    )
    got = made(
        functools.partial(second_kernel, shift),
        "second",
        {
            "v0": joined["x"],
            "left": left_env,
            "earlier": earlier,
            "factor": earlier_factor,
            "token": renewed["token"],
            **common,
        },
        {"env": struct((terms, held, cap, cap), BF16), **local_outs},
        flops=one * 52,
    )
    basis, lines = relaxed(joined["x"], came, got, got["env"])
    done = made(
        functools.partial(finish_kernel, shift),
        "finish",
        {"facts": facts, "lines": lines, **basis},
        {"x": struct(psi.shape, F32), "energy": struct((1,), F32)},
    )
    return (done["x"], done["energy"], renewed["out"])


def solution(mesh):
    return jax.shard_map(
        body,
        mesh=mesh,
        in_specs=(
            P("seg", "sec", None, None),
            P("seg", None, "sec", None, None),
            P("seg", None, "sec", None, None),
            P("seg", None, "sec", None, None),
            P("seg", None, "sec", None, None),
            P("seg", None),
        ),
        out_specs=(P("seg", "sec", None, None), P("seg"), P("seg", None, "sec", None, None)),
        check_vma=False,
    )
```

```python
import functools

import jax
import jax.numpy as jnp
from jax import lax
from jax.experimental import pallas as pl
from jax.experimental.pallas import tpu as pltpu
from jax.sharding import PartitionSpec as P

ITERS = 4
TAU = 0.05
F32 = jnp.float32
BF16 = jnp.bfloat16
LANES = 128
VMEM_LIMIT = 24 << 20
ROWS = 8

VMEM = pl.BlockSpec(memory_space=pltpu.VMEM)
SMEM = pl.BlockSpec(memory_space=pltpu.SMEM)
HBM = pl.BlockSpec(memory_space=pltpu.HBM)


def nn(a, b):
    return lax.dot_general(a, b, (((1,), (0,)), ((), ())), preferred_element_type=F32)


def nt(a, b):
    return lax.dot_general(a, b, (((1,), (1,)), ((), ())), preferred_element_type=F32)


def hop(block, inner, outer):
    return nn(outer, nt(block, inner).astype(BF16))


def masked(block, dim):
    rows = lax.broadcasted_iota(jnp.int32, block.shape, 0)
    cols = lax.broadcasted_iota(jnp.int32, block.shape, 1)
    return jnp.where(jnp.logical_and(rows < dim, cols < dim), block, 0.0)


def local_part(v, env, right, outer, inner, shift, ready=lambda *what: None):
    held = len(v)
    terms = right.shape[1]
    b = [x.astype(BF16) for x in v]
    half = []
    for w in range(terms):
        ready("right", w)
        half.append([nt(b[s], right[0, w, s]).astype(BF16) for s in range(held)])
    image = [None] * held
    ready("hops")
    for s in range(held):
        if s > 0:
            image[s] = hop(b[s - 1], inner[0, 0, s], outer[0, 0, s])
        if s + 1 < held:
            above = hop(b[s + 1], inner[0, 1, s], outer[0, 1, s])
            image[s] = above if image[s] is None else image[s] + above
    for w in range(terms):
        ready("left", w)
        for s in range(held):
            term = nn(env(w, s), half[w][s])
            image[s] = term if image[s] is None else image[s] + term
    return [v[s] * (1.0 + TAU * shift) - TAU * image[s] for s in range(held)]


def dot_rows(basis, last):
    rows = lax.broadcasted_iota(jnp.int32, (ROWS, LANES), 0)
    out = jnp.zeros((ROWS, LANES), F32)
    for i, other in enumerate(basis):
        total = sum(jnp.sum(a * b, axis=0, keepdims=True) for a, b in zip(other, last))
        total = sum(total[:, n : n + LANES] for n in range(0, total.shape[1], LANES))
        out = jnp.where(rows == i, total, out)
    return out


class Facts:
    ODD, FIRST, LIVE, INSIDE, ACROSS, DIM = range(6)

    def __init__(self, ref):
        self.ref = ref

    def row(self, n):
        return self.ref[n : n + 1, 0:1]

    @property
    def odd(self):
        return self.row(self.ODD) == 1

    def dim(self, s):
        return self.row(self.DIM + s)


def swapped(odd, low, high):
    return jnp.where(odd, low, high), jnp.where(odd, high, low)


def start_kernel(
    place, dims_at, psi_at, outer_at, inner_at, v0, inside, across, facts, dims, psi, blocks, arrived
):
    held, cap, _ = psi.shape
    known = pltpu.make_async_copy(dims_at, dims, arrived.at[held + 4])
    known.start()
    copies = [pltpu.make_async_copy(psi_at.at[0, s], psi.at[s], arrived.at[s]) for s in range(held)]
    for n, (side, s) in enumerate(((0, 0), (1, held - 1))):
        for m, array in enumerate((outer_at, inner_at)):
            copies.append(
                pltpu.make_async_copy(
                    array.at[0, side, s], blocks.at[2 * n + m], arrived.at[held + 2 * n + m]
                )
            )
    for copy in copies:
        copy.start()
    known.wait()
    first = place[0] * held
    last = dims.shape[1] - 1
    odd = place[0] % 2
    low_dim = dims[0, jnp.maximum(first - 1, 0)]
    high_dim = dims[0, jnp.minimum(first + held, last)]
    live = jnp.int32(0)
    for s in range(dims.shape[1]):
        live = live + dims[0, s] * dims[0, s]
    rows = [
        odd,
        jnp.where(place[1] == 0, 1, 0),
        live,
        jnp.where(odd == 1, low_dim, high_dim),
        jnp.where(odd == 1, high_dim, low_dim),
    ] + [dims[0, first + s] for s in range(held)]
    for n, value in enumerate(rows):
        facts[n : n + 1, :] = jnp.full((1, LANES), value, jnp.int32)
    for copy in copies[:held]:
        copy.wait()
    edges = [masked(psi[s], dims[0, first + s]) for s in range(held)]
    for s in range(held):
        v0[s] = edges[s]
    low = edges[0].astype(BF16)
    high = edges[-1].astype(BF16)
    inside[0] = jnp.where(odd == 1, low, high)
    across[0] = jnp.where(odd == 1, high, low)
    for copy in copies[held:]:
        copy.wait()
    for m in range(2):
        inside[1 + m] = jnp.where(odd == 1, blocks[m], blocks[2 + m])
        across[1 + m] = jnp.where(odd == 1, blocks[2 + m], blocks[m])


def put_local(v, env, r, shift, **ready):
    facts = Facts(r["facts"])
    out = local_part(v, env, r["right"], r["outer"], r["inner"], shift, **ready)
    for s, block in enumerate(out):
        r["q"][s] = block
    if "inside" not in r:
        return
    inside, across = swapped(facts.odd, out[0], out[-1])
    r["inside"][...] = inside.astype(BF16)
    r["across"][...] = across.astype(BF16)


def local_kernel(shift, names, *refs):
    r = dict(zip(names, refs))
    arrived = refs[-1]
    copies = {}
    for n in ("outer", "inner"):
        copies[n] = pltpu.make_async_copy(r[n + "_at"], r[n], arrived.at[len(copies)])
    for n in ("right", "left"):
        for w in range(r[n].shape[1]):
            copies[n, w] = pltpu.make_async_copy(
                r[n + "_at"].at[0, w], r[n].at[0, w], arrived.at[len(copies)]
            )
    order = [("right", w) for w in range(r["right"].shape[1])] + ["outer", "inner"]
    order += [("left", w) for w in range(r["left"].shape[1])]
    for key in order:
        copies[key].start()

    def ready(*what):
        for key in ("outer", "inner") if what == ("hops",) else (what,):
            copies[key].wait()

    v = [r["v0"][s] for s in range(r["v0"].shape[0])]
    put_local(v, lambda w, s: r["left"][0, w, s], r, shift, ready=ready)
    r["dots"][...] = dot_rows([v], v)


def ghosts(k, facts, r):
    came = [r["came_inside"], r["came_across"]]
    came = [(c[0] if len(c.shape) == 3 else c[...]).astype(F32) for c in came]
    if k > 0:
        before = r[f"v{k - 1}"]
        sent = swapped(facts.odd, before[0], before[before.shape[0] - 1])
        dims = (facts.row(facts.INSIDE), facts.row(facts.ACROSS))
        hops = (r["hops_inside"], r["hops_across"])
        came = [
            masked(c - TAU * hop(b.astype(BF16), h[2], h[1]), d)
            for c, b, h, d in zip(came, sent, hops, dims)
        ]
    low, high = swapped(facts.odd, *came)
    return low.astype(BF16), high.astype(BF16)


def step_kernel(k, shift, names, *refs):
    r = dict(zip(names, refs))
    facts = Facts(r["facts"])
    outer, inner = r["outer"], r["inner"]
    held = r["part"].shape[0]
    low, high = ghosts(k, facts, r)
    v = [r["part"][s] for s in range(held)]
    v[0] = v[0] - TAU * hop(low, inner[0, 0, 0], outer[0, 0, 0])
    v[-1] = v[-1] - TAU * hop(high, inner[0, 1, held - 1], outer[0, 1, held - 1])
    v = [masked(block, facts.dim(s)) for s, block in enumerate(v)]
    for s in range(held):
        r["v"][s] = v[s]
    basis = [[r[f"v{i}"][s] for s in range(held)] for i in range(k + 1)]
    if k + 1 < ITERS:
        left = r["left"]
        env = (lambda w, s: left[0, w, s]) if len(left.shape) == 5 else (lambda w, s: left[w, s])
        put_local(v, env, r, shift)
        r["dots"][...] = dot_rows(basis + [v], v)
    else:
        lanes = lax.broadcasted_iota(jnp.int32, (ROWS, LANES), 1)
        rows = lax.broadcasted_iota(jnp.int32, (ROWS, LANES), 0)
        line = jnp.zeros((1, LANES), F32)
        for j in range(ITERS + 1):
            part = r[f"dots{j}"][...] if j < ITERS else dot_rows(basis + [v], v)
            part = jnp.sum(part, axis=1, keepdims=True)
            line = line + jnp.sum(
                jnp.where(lanes == ROWS * j + rows, part, 0.0), axis=0, keepdims=True
            )
        for n in range(r["line"].shape[0]):
            r["line"][n] = line


def combination(line, live_count, shift):
    lanes = lax.broadcasted_iota(jnp.int32, (1, LANES), 1)
    gram = {}
    for j in range(ITERS + 1):
        for i in range(j + 1):
            gram[i, j] = jnp.sum(
                jnp.where(lanes == ROWS * j + i, line, 0.0), axis=1, keepdims=True
            )
            gram[j, i] = gram[i, j]
    coefs = [jnp.ones((1, 1), F32)]
    energy = None
    for _ in range(ITERS):
        n = len(coefs)
        onto = [sum(coefs[i] * gram[i, j] for i in range(n)) for j in range(n + 1)]
        raised = [sum(coefs[i] * gram[i + 1, j] for i in range(n)) for j in range(1, n + 1)]
        self_dot = sum(coefs[j] * onto[j] for j in range(n))
        cross = sum(coefs[j] * onto[j + 1] for j in range(n))
        square = sum(coefs[j] * raised[j] for j in range(n))
        ratio = cross / self_dot
        gain = 1.0 - ratio
        energy = shift + gain / TAU
        norm = square + gain * (2.0 * cross + gain * self_dot)
        scale = jnp.sqrt(live_count / norm)
        moved = [gain * c for c in coefs] + [jnp.zeros((1, 1), F32)]
        moved = [moved[0]] + [moved[i + 1] + coefs[i] for i in range(n)]
        coefs = [scale * c for c in moved]
    return coefs, energy


def join_kernel(shift, names, *refs):
    r = dict(zip(names, refs))
    facts = Facts(r["facts"])
    line = jnp.sum(r["lines"][...], axis=0)
    coefs, _ = combination(line, facts.row(facts.LIVE).astype(F32), shift)
    held, cap, _ = r["v0"].shape
    pad = r["factor"].shape[1] - cap
    blocks = [sum(c * r[f"v{k}"][s] for k, c in enumerate(coefs)) for s in range(held)]
    for s, block in enumerate(blocks):
        r["x"][s] = block
        r["factor"][s, :cap] = block.astype(BF16)
        dim = jnp.broadcast_to(facts.dim(s).astype(F32), (pad, cap))
        r["factor"][s, cap:] = dim.astype(BF16)
    inside, across = swapped(facts.odd, blocks[0], blocks[-1])
    r["inside"][...] = inside.astype(BF16)
    r["across"][...] = across.astype(BF16)


def grown(env, factor):
    cap = env.shape[0]
    block = factor[:cap]
    product = nn(block.T, nn(env, block).astype(BF16))
    return (product / factor[cap : cap + 1].astype(F32)).astype(BF16)


def grow_kernel(left, factor, out, token, held_out, sent):
    copies = []
    for w in range(left.shape[1]):
        for s in range(left.shape[2]):
            held_out[w, s] = grown(left[0, w, s], factor[s])
        copies.append(pltpu.make_async_copy(held_out.at[w], out.at[0, w], sent.at[w]))
        copies[-1].start()
    token[...] = jnp.zeros_like(token)
    for copy in copies:
        copy.wait()


def second_kernel(shift, names, *refs):
    r = dict(zip(names, refs))
    facts = Facts(r["facts"])
    held = r["v0"].shape[0]
    first = facts.row(facts.FIRST) == 1
    for s in range(held):
        for w in range(r["left"].shape[1]):
            new = grown(r["earlier"][0, w, s], r["factor"][s]).astype(F32)
            kept = r["left"][0, w, s].astype(F32)
            r["env"][w, s] = jnp.where(first, kept, new).astype(BF16)
    v = [r["v0"][s] for s in range(held)]
    put_local(v, lambda w, s: r["env"][w, s], r, shift)
    r["dots"][...] = dot_rows([v], v)


def finish_kernel(shift, names, *refs):
    r = dict(zip(names, refs))
    facts = Facts(r["facts"])
    line = jnp.sum(r["lines"][...], axis=0)
    coefs, energy = combination(line, facts.row(facts.LIVE).astype(F32), shift)
    held_out, sent = refs[-2:]
    copies = []
    for s in range(r["v0"].shape[0]):
        held_out[s] = sum(c * r[f"v{k}"][s] for k, c in enumerate(coefs))
        copies.append(pltpu.make_async_copy(held_out.at[s], r["x"].at[0, s], sent.at[s]))
        copies[-1].start()
    r["energy"][0] = energy[0, 0]
    for copy in copies:
        copy.wait()


def in_hbm(array):
    return pltpu.with_memory_space_constraint(array, pltpu.HBM)


def struct(shape, dtype):
    return jax.ShapeDtypeStruct(shape, dtype)


def call(kernel, name, ins, outs, flops=0, specs=None, scratch=(), outside=()):
    args = tuple(ins.values())
    values = pl.pallas_call(
        kernel,
        out_shape=tuple(outs.values()),
        in_specs=specs or [VMEM] * len(args),
        out_specs=tuple(
            SMEM if o.shape == (1,) else HBM if n in outside else VMEM for n, o in outs.items()
        ),
        scratch_shapes=scratch,
        name=name,
        compiler_params=pltpu.CompilerParams(vmem_limit_bytes=VMEM_LIMIT),
        cost_estimate=pl.CostEstimate(
            flops=flops,
            transcendentals=0,
            bytes_accessed=sum(a.size * a.dtype.itemsize for a in args),
        ),
    )(*args)
    return dict(zip(outs, values))


def body(psi, left_env, right_env, hop_outer, hop_inner, dims):
    _, terms, held, cap, _ = left_env.shape
    shift = float(terms)
    size = lax.axis_size("sec")
    place = jnp.stack([lax.axis_index("sec"), lax.axis_index("seg")]).astype(jnp.int32)
    block = struct((cap, cap), BF16)
    blocks = struct((held, cap, cap), F32)
    triple = struct((3, cap, cap), BF16)
    dots_of = struct((ROWS, LANES), F32)
    local_outs = {"q": blocks, "inside": block, "across": block, "dots": dots_of}
    pairs = [(i, i ^ 1) for i in range(size)]
    others = [(i, i + 1 if i % 2 else i - 1) for i in range(1, size - 1)]
    onward = [(i, i + 1) for i in range(lax.axis_size("seg") - 1)]
    one = 2 * cap**3

    def exchange(got):
        return {
            "came_inside": lax.ppermute(got["inside"], "sec", pairs),
            "came_across": lax.ppermute(got["across"], "sec", others),
        }

    def made(kernel, name, ins, outs, flops=0, **more):
        names = tuple(ins) + tuple(outs)
        return call(functools.partial(kernel, names), name, ins, outs, flops, **more)

    start = call(
        start_kernel,
        "start",
        {
            "place": place,
            "dims": in_hbm(dims),
            "psi": in_hbm(psi),
            "outer": in_hbm(hop_outer),
            "inner": in_hbm(hop_inner),
        },
        {
            "v0": blocks,
            "inside": triple,
            "across": triple,
            "facts": struct((ROWS * (1 + (4 + held) // ROWS), LANES), jnp.int32),
        },
        specs=[SMEM, HBM, HBM, HBM, HBM],
        scratch=[
            pltpu.SMEM(dims.shape, jnp.int32),
            pltpu.VMEM((held, cap, cap), F32),
            pltpu.VMEM((4, cap, cap), BF16),
            pltpu.SemaphoreType.DMA((held + 5,)),
        ],
    )
    facts = start["facts"]
    came = exchange(start)
    hops = {"hops_inside": came["came_inside"], "hops_across": came["came_across"]}
    earlier = lax.ppermute(left_env, "seg", onward)

    def relaxed(v0, came, got, env):
        basis = {"v0": v0}
        dots = {"dots0": got["dots"]}
        for k in range(ITERS):
            ins = {"part": got["q"], **common, **basis, **came}
            if k > 0:
                ins.update(hops)
            if k + 1 < ITERS:
                came = exchange(got)
                ins.update(left=env)
                outs = {"v": blocks, **local_outs}
                if k + 2 == ITERS:
                    del outs["inside"], outs["across"]
            else:
                del ins["right"]
                ins.update(dots)
                outs = {"v": blocks, "line": struct((size, 1, LANES), F32)}
            kernel = functools.partial(step_kernel, k, shift)
            got = made(kernel, f"step{k}", ins, outs, flops=one * 36)
            basis[f"v{k + 1}"] = got["v"]
            if k + 1 < ITERS:
                dots[f"dots{k + 1}"] = got["dots"]
        return basis, lax.all_to_all(got["line"], "sec", 0, 0)

    got = made(
        functools.partial(local_kernel, shift),
        "local",
        {
            "facts": facts,
            "v0": start["v0"],
            "left_at": in_hbm(left_env),
            "right_at": in_hbm(right_env),
            "outer_at": in_hbm(hop_outer),
            "inner_at": in_hbm(hop_inner),
        },
        {
            "left": struct(left_env.shape, BF16),
            "right": struct(right_env.shape, BF16),
            "outer": struct(hop_outer.shape, BF16),
            "inner": struct(hop_inner.shape, BF16),
            **local_outs,
        },
        flops=one * 28,
        specs=[VMEM, VMEM, HBM, HBM, HBM, HBM],
        scratch=[pltpu.SemaphoreType.DMA((2 + 2 * terms,))],
    )
    left = got["left"]
    common = {"facts": facts, **{n: got[n] for n in ("outer", "inner", "right")}}
    basis, lines = relaxed(start["v0"], came, got, left)
    joined = made(
        functools.partial(join_kernel, shift),
        "join",
        {"facts": facts, "lines": lines, **basis},
        {
            "x": blocks,
            "factor": struct((held, cap + 16, cap), BF16),
            "inside": block,
            "across": block,
        },
    )
    factor = joined["factor"]
    earlier_factor = lax.ppermute(factor, "seg", onward)
    came = exchange(joined)
    renewed = call(
        grow_kernel,
        "grow",
        {"left": left, "factor": factor},
        {"out": struct(left_env.shape, BF16), "token": dots_of},
        flops=one * 24,
        scratch=[
            pltpu.VMEM((terms, held, cap, cap), BF16),
            pltpu.SemaphoreType.DMA((terms,)),
        ],
        outside=("out",),
    )
    got = made(
        functools.partial(second_kernel, shift),
        "second",
        {
            "v0": joined["x"],
            "left": left,
            "earlier": earlier,
            "factor": earlier_factor,
            "token": renewed["token"],
            **common,
        },
        {"env": struct((terms, held, cap, cap), BF16), **local_outs},
        flops=one * 52,
    )
    basis, lines = relaxed(joined["x"], came, got, got["env"])
    done = made(
        functools.partial(finish_kernel, shift),
        "finish",
        {"facts": facts, "lines": lines, **basis},
        {"x": struct(psi.shape, F32), "energy": struct((1,), F32)},
        scratch=[pltpu.VMEM((held, cap, cap), F32), pltpu.SemaphoreType.DMA((held,))],
        outside=("x",),
    )
    return (done["x"], done["energy"], renewed["out"])


def solution(mesh):
    return jax.shard_map(
        body,
        mesh=mesh,
        in_specs=(
            P("seg", "sec", None, None),
            P("seg", None, "sec", None, None),
            P("seg", None, "sec", None, None),
            P("seg", None, "sec", None, None),
            P("seg", None, "sec", None, None),
            P("seg", None),
        ),
        out_specs=(P("seg", "sec", None, None), P("seg"), P("seg", None, "sec", None, None)),
        check_vma=False,
    )
```

```python
import functools

import jax
import jax.numpy as jnp
from jax import lax
from jax.experimental import pallas as pl
from jax.experimental.pallas import tpu as pltpu
from jax.sharding import PartitionSpec as P

ITERS = 4
TAU = 0.05
F32 = jnp.float32
BF16 = jnp.bfloat16
LANES = 128
VMEM_LIMIT = 24 << 20
ROWS = 8

VMEM = pl.BlockSpec(memory_space=pltpu.VMEM)
SMEM = pl.BlockSpec(memory_space=pltpu.SMEM)
HBM = pl.BlockSpec(memory_space=pltpu.HBM)


def nn(a, b):
    return lax.dot_general(a, b, (((1,), (0,)), ((), ())), preferred_element_type=F32)


def nt(a, b):
    return lax.dot_general(a, b, (((1,), (1,)), ((), ())), preferred_element_type=F32)


def hop(block, inner, outer):
    return nn(outer, nt(block, inner).astype(BF16))


def masked(block, dim):
    rows = lax.broadcasted_iota(jnp.int32, block.shape, 0)
    cols = lax.broadcasted_iota(jnp.int32, block.shape, 1)
    return jnp.where(jnp.logical_and(rows < dim, cols < dim), block, 0.0)


def local_part(v, env, right, outer, inner, shift, ready=lambda *what: None):
    held = len(v)
    terms = right.shape[1]
    b = [x.astype(BF16) for x in v]
    half = []
    for w in range(terms):
        ready("right", w)
        half.append([nt(b[s], right[0, w, s]).astype(BF16) for s in range(held)])
    image = [None] * held
    ready("hops")
    for s in range(held):
        if s > 0:
            image[s] = hop(b[s - 1], inner[0, 0, s], outer[0, 0, s])
        if s + 1 < held:
            above = hop(b[s + 1], inner[0, 1, s], outer[0, 1, s])
            image[s] = above if image[s] is None else image[s] + above
    for w in range(terms):
        ready("left", w)
        for s in range(held):
            term = nn(env(w, s), half[w][s])
            image[s] = term if image[s] is None else image[s] + term
    return [v[s] * (1.0 + TAU * shift) - TAU * image[s] for s in range(held)]


def dot_rows(basis, last):
    rows = lax.broadcasted_iota(jnp.int32, (ROWS, LANES), 0)
    out = jnp.zeros((ROWS, LANES), F32)
    for i, other in enumerate(basis):
        total = sum(jnp.sum(a * b, axis=0, keepdims=True) for a, b in zip(other, last))
        total = sum(total[:, n : n + LANES] for n in range(0, total.shape[1], LANES))
        out = jnp.where(rows == i, total, out)
    return out


class Facts:
    ODD, FIRST, LIVE, INSIDE, ACROSS, DIM = range(6)

    def __init__(self, ref):
        self.ref = ref

    def row(self, n):
        return self.ref[n : n + 1, 0:1]

    @property
    def odd(self):
        return self.row(self.ODD) == 1

    def dim(self, s):
        return self.row(self.DIM + s)


def swapped(odd, low, high):
    return jnp.where(odd, low, high), jnp.where(odd, high, low)


def start_kernel(
    place, dims_at, psi_at, outer_at, inner_at, v0, inside, across, facts, dims, psi, blocks, arrived
):
    held, cap, _ = psi.shape
    known = pltpu.make_async_copy(dims_at, dims, arrived.at[held + 4])
    known.start()
    copies = [pltpu.make_async_copy(psi_at.at[0, s], psi.at[s], arrived.at[s]) for s in range(held)]
    for n, (side, s) in enumerate(((0, 0), (1, held - 1))):
        for m, array in enumerate((outer_at, inner_at)):
            copies.append(
                pltpu.make_async_copy(
                    array.at[0, side, s], blocks.at[2 * n + m], arrived.at[held + 2 * n + m]
                )
            )
    for copy in copies:
        copy.start()
    known.wait()
    first = place[0] * held
    last = dims.shape[1] - 1
    odd = place[0] % 2
    low_dim = jnp.where(first == 0, 0, dims[0, jnp.maximum(first - 1, 0)])
    high_dim = jnp.where(first + held > last, 0, dims[0, jnp.minimum(first + held, last)])
    live = jnp.int32(0)
    for s in range(dims.shape[1]):
        live = live + dims[0, s] * dims[0, s]
    rows = [
        odd,
        jnp.where(place[1] == 0, 1, 0),
        live,
        jnp.where(odd == 1, low_dim, high_dim),
        jnp.where(odd == 1, high_dim, low_dim),
    ] + [dims[0, first + s] for s in range(held)]
    for n, value in enumerate(rows):
        facts[n : n + 1, :] = jnp.full((1, LANES), value, jnp.int32)
    for copy in copies[:held]:
        copy.wait()
    edges = [masked(psi[s], dims[0, first + s]) for s in range(held)]
    for s in range(held):
        v0[s] = edges[s]
    low = edges[0].astype(BF16)
    high = edges[-1].astype(BF16)
    inside[0] = jnp.where(odd == 1, low, high)
    across[0] = jnp.where(odd == 1, high, low)
    for copy in copies[held:]:
        copy.wait()
    for m in range(2):
        inside[1 + m] = jnp.where(odd == 1, blocks[m], blocks[2 + m])
        across[1 + m] = jnp.where(odd == 1, blocks[2 + m], blocks[m])


def put_local(v, env, r, shift, **ready):
    facts = Facts(r["facts"])
    out = local_part(v, env, r["right"], r["outer"], r["inner"], shift, **ready)
    for s, block in enumerate(out):
        r["q"][s] = block
    if "inside" not in r:
        return
    inside, across = swapped(facts.odd, out[0], out[-1])
    r["inside"][...] = inside.astype(BF16)
    r["across"][...] = across.astype(BF16)


def local_kernel(shift, names, *refs):
    r = dict(zip(names, refs))
    arrived = refs[-1]
    copies = {}
    for n in ("outer", "inner"):
        copies[n] = pltpu.make_async_copy(r[n + "_at"], r[n], arrived.at[len(copies)])
    for n in ("right", "left"):
        for w in range(r[n].shape[1]):
            copies[n, w] = pltpu.make_async_copy(
                r[n + "_at"].at[0, w], r[n].at[0, w], arrived.at[len(copies)]
            )
    order = [("right", w) for w in range(r["right"].shape[1])] + ["outer", "inner"]
    order += [("left", w) for w in range(r["left"].shape[1])]
    for key in order:
        copies[key].start()

    def ready(*what):
        for key in ("outer", "inner") if what == ("hops",) else (what,):
            copies[key].wait()

    v = [r["v0"][s] for s in range(r["v0"].shape[0])]
    put_local(v, lambda w, s: r["left"][0, w, s], r, shift, ready=ready)
    r["dots"][...] = dot_rows([v], v)


def ghosts(k, facts, r):
    came = []
    for n, (name, row) in enumerate((("inside", facts.INSIDE), ("across", facts.ACROSS))):
        ref = r["came_" + name]
        block = (ref[0] if len(ref.shape) == 3 else ref[...]).astype(F32)
        if k > 0:
            block = block - r["given"][n]
        came.append(masked(block, facts.row(row)))
    low, high = swapped(facts.odd, *came)
    return low.astype(BF16), high.astype(BF16)


def put_given(v, facts, r):
    sent = swapped(facts.odd, v[0], v[-1])
    for n, (block, name) in enumerate(zip(sent, ("hops_inside", "hops_across"))):
        r["gives"][n] = TAU * hop(block.astype(BF16), r[name][2], r[name][1])


def step_kernel(k, shift, names, *refs):
    r = dict(zip(names, refs))
    facts = Facts(r["facts"])
    outer, inner = r["outer"], r["inner"]
    held = r["part"].shape[0]
    low, high = ghosts(k, facts, r)
    v = [r["part"][s] for s in range(held)]
    v[0] = v[0] - TAU * hop(low, inner[0, 0, 0], outer[0, 0, 0])
    v[-1] = v[-1] - TAU * hop(high, inner[0, 1, held - 1], outer[0, 1, held - 1])
    v = [masked(block, facts.dim(s)) for s, block in enumerate(v)]
    for s in range(held):
        r["v"][s] = v[s]
    basis = [[r[f"v{i}"][s] for s in range(held)] for i in range(k + 1)]
    if k + 1 < ITERS:
        put_given(basis[k], facts, r)
        left = r["left"]
        env = (lambda w, s: left[0, w, s]) if len(left.shape) == 5 else (lambda w, s: left[w, s])
        put_local(v, env, r, shift)
        r["dots"][...] = dot_rows(basis + [v], v)
    else:
        lanes = lax.broadcasted_iota(jnp.int32, (ROWS, LANES), 1)
        rows = lax.broadcasted_iota(jnp.int32, (ROWS, LANES), 0)
        line = jnp.zeros((1, LANES), F32)
        for j in range(ITERS + 1):
            part = r[f"dots{j}"][...] if j < ITERS else dot_rows(basis + [v], v)
            part = jnp.sum(part, axis=1, keepdims=True)
            line = line + jnp.sum(
                jnp.where(lanes == ROWS * j + rows, part, 0.0), axis=0, keepdims=True
            )
        for n in range(r["line"].shape[0]):
            r["line"][n] = line


def combination(line, live_count, shift):
    lanes = lax.broadcasted_iota(jnp.int32, (1, LANES), 1)
    gram = {}
    for j in range(ITERS + 1):
        for i in range(j + 1):
            gram[i, j] = jnp.sum(
                jnp.where(lanes == ROWS * j + i, line, 0.0), axis=1, keepdims=True
            )
            gram[j, i] = gram[i, j]
    coefs = [jnp.ones((1, 1), F32)]
    energy = None
    for _ in range(ITERS):
        n = len(coefs)
        onto = [sum(coefs[i] * gram[i, j] for i in range(n)) for j in range(n + 1)]
        raised = [sum(coefs[i] * gram[i + 1, j] for i in range(n)) for j in range(1, n + 1)]
        self_dot = sum(coefs[j] * onto[j] for j in range(n))
        cross = sum(coefs[j] * onto[j + 1] for j in range(n))
        square = sum(coefs[j] * raised[j] for j in range(n))
        ratio = cross / self_dot
        gain = 1.0 - ratio
        energy = shift + gain / TAU
        norm = square + gain * (2.0 * cross + gain * self_dot)
        scale = jnp.sqrt(live_count / norm)
        moved = [gain * c for c in coefs] + [jnp.zeros((1, 1), F32)]
        moved = [moved[0]] + [moved[i + 1] + coefs[i] for i in range(n)]
        coefs = [scale * c for c in moved]
    return coefs, energy


def join_kernel(shift, names, *refs):
    r = dict(zip(names, refs))
    facts = Facts(r["facts"])
    line = jnp.sum(r["lines"][...], axis=0)
    coefs, _ = combination(line, facts.row(facts.LIVE).astype(F32), shift)
    held, cap, _ = r["v0"].shape
    pad = r["factor"].shape[1] - cap
    blocks = [sum(c * r[f"v{k}"][s] for k, c in enumerate(coefs)) for s in range(held)]
    for s, block in enumerate(blocks):
        r["x"][s] = block
        r["factor"][s, :cap] = block.astype(BF16)
        dim = jnp.broadcast_to(facts.dim(s).astype(F32), (pad, cap))
        r["factor"][s, cap:] = dim.astype(BF16)
    inside, across = swapped(facts.odd, blocks[0], blocks[-1])
    r["inside"][...] = inside.astype(BF16)
    r["across"][...] = across.astype(BF16)


def grown(env, factor):
    cap = env.shape[0]
    block = factor[:cap]
    product = nn(block.T, nn(env, block).astype(BF16))
    return (product / factor[cap : cap + 1].astype(F32)).astype(BF16)


def grow_kernel(left, factor, out, token, held_out, sent):
    copies = []
    for w in range(left.shape[1]):
        for s in range(left.shape[2]):
            held_out[w, s] = grown(left[0, w, s], factor[s])
        copies.append(pltpu.make_async_copy(held_out.at[w], out.at[0, w], sent.at[w]))
        copies[-1].start()
    token[...] = jnp.zeros_like(token)
    for copy in copies:
        copy.wait()


def second_kernel(shift, names, *refs):
    r = dict(zip(names, refs))
    facts = Facts(r["facts"])
    held = r["v0"].shape[0]
    first = facts.row(facts.FIRST) == 1
    for s in range(held):
        for w in range(r["left"].shape[1]):
            new = grown(r["earlier"][0, w, s], r["factor"][s]).astype(F32)
            kept = r["left"][0, w, s].astype(F32)
            r["env"][w, s] = jnp.where(first, kept, new).astype(BF16)
    v = [r["v0"][s] for s in range(held)]
    put_local(v, lambda w, s: r["env"][w, s], r, shift)
    r["dots"][...] = dot_rows([v], v)


def finish_kernel(shift, names, *refs):
    r = dict(zip(names, refs))
    facts = Facts(r["facts"])
    line = jnp.sum(r["lines"][...], axis=0)
    coefs, energy = combination(line, facts.row(facts.LIVE).astype(F32), shift)
    for s in range(r["v0"].shape[0]):
        r["x"][0, s] = sum(c * r[f"v{k}"][s] for k, c in enumerate(coefs))
    r["energy"][0] = energy[0, 0]


def in_hbm(array):
    return pltpu.with_memory_space_constraint(array, pltpu.HBM)


def struct(shape, dtype):
    return jax.ShapeDtypeStruct(shape, dtype)


def call(kernel, name, ins, outs, flops=0, specs=None, scratch=(), outside=()):
    args = tuple(ins.values())
    values = pl.pallas_call(
        kernel,
        out_shape=tuple(outs.values()),
        in_specs=specs or [VMEM] * len(args),
        out_specs=tuple(
            SMEM if o.shape == (1,) else HBM if n in outside else VMEM for n, o in outs.items()
        ),
        scratch_shapes=scratch,
        name=name,
        compiler_params=pltpu.CompilerParams(vmem_limit_bytes=VMEM_LIMIT),
        cost_estimate=pl.CostEstimate(
            flops=flops,
            transcendentals=0,
            bytes_accessed=sum(a.size * a.dtype.itemsize for a in args),
        ),
    )(*args)
    return dict(zip(outs, values))


def body(psi, left_env, right_env, hop_outer, hop_inner, dims):
    _, terms, held, cap, _ = left_env.shape
    shift = float(terms)
    size = lax.axis_size("sec")
    place = jnp.stack([lax.axis_index("sec"), lax.axis_index("seg")]).astype(jnp.int32)
    block = struct((cap, cap), BF16)
    blocks = struct((held, cap, cap), F32)
    pair = struct((2, cap, cap), F32)
    triple = struct((3, cap, cap), BF16)
    dots_of = struct((ROWS, LANES), F32)
    local_outs = {"q": blocks, "inside": block, "across": block, "dots": dots_of}
    pairs = [(i, i ^ 1) for i in range(size)]
    others = [(i, min(i + 1, size - 1) if i % 2 else max(i - 1, 0)) for i in range(size)]
    segments = lax.axis_size("seg")
    onward = [(i, (i + 1) % segments) for i in range(segments)]
    one = 2 * cap**3

    def exchange(got):
        return {
            "came_inside": lax.ppermute(got["inside"], "sec", pairs),
            "came_across": lax.ppermute(got["across"], "sec", others),
        }

    def made(kernel, name, ins, outs, flops=0, **more):
        names = tuple(ins) + tuple(outs)
        return call(functools.partial(kernel, names), name, ins, outs, flops, **more)

    start = call(
        start_kernel,
        "start",
        {
            "place": place,
            "dims": in_hbm(dims),
            "psi": in_hbm(psi),
            "outer": in_hbm(hop_outer),
            "inner": in_hbm(hop_inner),
        },
        {
            "v0": blocks,
            "inside": triple,
            "across": triple,
            "facts": struct((ROWS * (1 + (4 + held) // ROWS), LANES), jnp.int32),
        },
        specs=[SMEM, HBM, HBM, HBM, HBM],
        scratch=[
            pltpu.SMEM(dims.shape, jnp.int32),
            pltpu.VMEM((held, cap, cap), F32),
            pltpu.VMEM((4, cap, cap), BF16),
            pltpu.SemaphoreType.DMA((held + 5,)),
        ],
    )
    facts = start["facts"]
    came = exchange(start)
    hops = {"hops_inside": came["came_inside"], "hops_across": came["came_across"]}
    earlier = lax.ppermute(left_env, "seg", onward)

    def relaxed(v0, came, got, env):
        basis = {"v0": v0}
        dots = {"dots0": got["dots"]}
        for k in range(ITERS):
            ins = {"part": got["q"], **common, **basis, **came}
            if k > 0:
                ins["given"] = got["gives"]
            if k + 1 < ITERS:
                came = exchange(got)
                ins.update(left=env, **hops)
                outs = {"v": blocks, "gives": pair, **local_outs}
                if k + 2 == ITERS:
                    del outs["inside"], outs["across"]
            else:
                del ins["right"]
                ins.update(dots)
                outs = {"v": blocks, "line": struct((size, 1, LANES), F32)}
            kernel = functools.partial(step_kernel, k, shift)
            got = made(kernel, f"step{k}", ins, outs, flops=one * 36)
            basis[f"v{k + 1}"] = got["v"]
            if k + 1 < ITERS:
                dots[f"dots{k + 1}"] = got["dots"]
        return basis, lax.all_to_all(got["line"], "sec", 0, 0)

    got = made(
        functools.partial(local_kernel, shift),
        "local",
        {
            "facts": facts,
            "v0": start["v0"],
            "left_at": in_hbm(left_env),
            "right_at": in_hbm(right_env),
            "outer_at": in_hbm(hop_outer),
            "inner_at": in_hbm(hop_inner),
        },
        {
            "left": struct(left_env.shape, BF16),
            "right": struct(right_env.shape, BF16),
            "outer": struct(hop_outer.shape, BF16),
            "inner": struct(hop_inner.shape, BF16),
            **local_outs,
        },
        flops=one * 28,
        specs=[VMEM, VMEM, HBM, HBM, HBM, HBM],
        scratch=[pltpu.SemaphoreType.DMA((2 + 2 * terms,))],
    )
    left = got["left"]
    common = {"facts": facts, **{n: got[n] for n in ("outer", "inner", "right")}}
    basis, lines = relaxed(start["v0"], came, got, left)
    joined = made(
        functools.partial(join_kernel, shift),
        "join",
        {"facts": facts, "lines": lines, **basis},
        {
            "x": blocks,
            "factor": struct((held, cap + 16, cap), BF16),
            "inside": block,
            "across": block,
        },
    )
    factor = joined["factor"]
    earlier_factor = lax.ppermute(factor, "seg", onward)
    came = exchange(joined)
    renewed = call(
        grow_kernel,
        "grow",
        {"left": left, "factor": factor},
        {"out": struct(left_env.shape, BF16), "token": dots_of},
        flops=one * 24,
        scratch=[
            pltpu.VMEM((terms, held, cap, cap), BF16),
            pltpu.SemaphoreType.DMA((terms,)),
        ],
        outside=("out",),
    )
    got = made(
        functools.partial(second_kernel, shift),
        "second",
        {
            "v0": joined["x"],
            "left": left,
            "earlier": earlier,
            "factor": earlier_factor,
            "token": renewed["token"],
            **common,
        },
        {"env": struct((terms, held, cap, cap), BF16), **local_outs},
        flops=one * 52,
    )
    basis, lines = relaxed(joined["x"], came, got, got["env"])
    done = made(
        functools.partial(finish_kernel, shift),
        "finish",
        {"facts": facts, "lines": lines, **basis},
        {"x": struct(psi.shape, F32), "energy": struct((1,), F32)},
    )
    return (done["x"], done["energy"], renewed["out"])


def solution(mesh):
    return jax.shard_map(
        body,
        mesh=mesh,
        in_specs=(
            P("seg", "sec", None, None),
            P("seg", None, "sec", None, None),
            P("seg", None, "sec", None, None),
            P("seg", None, "sec", None, None),
            P("seg", None, "sec", None, None),
            P("seg", None),
        ),
        out_specs=(P("seg", "sec", None, None), P("seg"), P("seg", None, "sec", None, None)),
        check_vma=False,
    )
```

```python
import functools

import jax
import jax.numpy as jnp
from jax import lax
from jax.experimental import pallas as pl
from jax.experimental.pallas import tpu as pltpu
from jax.sharding import PartitionSpec as P

ITERS = 4
TAU = 0.05
F32 = jnp.float32
BF16 = jnp.bfloat16
LANES = 128
VMEM_LIMIT = 24 << 20
ROWS = 8

VMEM = pl.BlockSpec(memory_space=pltpu.VMEM)
SMEM = pl.BlockSpec(memory_space=pltpu.SMEM)
HBM = pl.BlockSpec(memory_space=pltpu.HBM)


def nn(a, b):
    return lax.dot_general(a, b, (((1,), (0,)), ((), ())), preferred_element_type=F32)


def nt(a, b):
    return lax.dot_general(a, b, (((1,), (1,)), ((), ())), preferred_element_type=F32)


def hop(block, inner, outer):
    return nn(outer, nt(block, inner).astype(BF16))


def masked(block, dim):
    rows = lax.broadcasted_iota(jnp.int32, block.shape, 0)
    cols = lax.broadcasted_iota(jnp.int32, block.shape, 1)
    return jnp.where(jnp.logical_and(rows < dim, cols < dim), block, 0.0)


def local_part(v, env, right, outer, inner, shift, ready=lambda *what: None):
    held = len(v)
    terms = right.shape[1]
    b = [x.astype(BF16) for x in v]
    half = []
    for w in range(terms):
        ready("right", w)
        half.append([nt(b[s], right[0, w, s]).astype(BF16) for s in range(held)])
    image = [None] * held
    ready("hops")
    for s in range(held):
        if s > 0:
            image[s] = hop(b[s - 1], inner[0, 0, s], outer[0, 0, s])
        if s + 1 < held:
            above = hop(b[s + 1], inner[0, 1, s], outer[0, 1, s])
            image[s] = above if image[s] is None else image[s] + above
    for w in range(terms):
        ready("left", w)
        for s in range(held):
            term = nn(env(w, s), half[w][s])
            image[s] = term if image[s] is None else image[s] + term
    return [v[s] * (1.0 + TAU * shift) - TAU * image[s] for s in range(held)]


def dot_rows(basis, last):
    rows = lax.broadcasted_iota(jnp.int32, (ROWS, LANES), 0)
    out = jnp.zeros((ROWS, LANES), F32)
    for i, other in enumerate(basis):
        total = sum(jnp.sum(a * b, axis=0, keepdims=True) for a, b in zip(other, last))
        total = sum(total[:, n : n + LANES] for n in range(0, total.shape[1], LANES))
        out = jnp.where(rows == i, total, out)
    return out


class Facts:
    ODD, FIRST, LIVE, INSIDE, ACROSS, DIM = range(6)

    def __init__(self, ref):
        self.ref = ref

    def row(self, n):
        return self.ref[n : n + 1, 0:1]

    @property
    def odd(self):
        return self.row(self.ODD) == 1

    def dim(self, s):
        return self.row(self.DIM + s)


def swapped(odd, low, high):
    return jnp.where(odd, low, high), jnp.where(odd, high, low)


def start_kernel(
    place, dims_at, psi_at, outer_at, inner_at, v0, inside, across, facts, dims, psi, blocks, arrived
):
    held, cap, _ = psi.shape
    known = pltpu.make_async_copy(dims_at, dims, arrived.at[held + 4])
    known.start()
    copies = [pltpu.make_async_copy(psi_at.at[0, s], psi.at[s], arrived.at[s]) for s in range(held)]
    for n, (side, s) in enumerate(((0, 0), (1, held - 1))):
        for m, array in enumerate((outer_at, inner_at)):
            copies.append(
                pltpu.make_async_copy(
                    array.at[0, side, s], blocks.at[2 * n + m], arrived.at[held + 2 * n + m]
                )
            )
    for copy in copies:
        copy.start()
    known.wait()
    first = place[0] * held
    last = dims.shape[1] - 1
    odd = place[0] % 2
    low_dim = jnp.where(first == 0, 0, dims[0, jnp.maximum(first - 1, 0)])
    high_dim = jnp.where(first + held > last, 0, dims[0, jnp.minimum(first + held, last)])
    live = jnp.int32(0)
    for s in range(dims.shape[1]):
        live = live + dims[0, s] * dims[0, s]
    rows = [
        odd,
        jnp.where(place[1] == 0, 1, 0),
        live,
        jnp.where(odd == 1, low_dim, high_dim),
        jnp.where(odd == 1, high_dim, low_dim),
    ] + [dims[0, first + s] for s in range(held)]
    for n, value in enumerate(rows):
        facts[n : n + 1, :] = jnp.full((1, LANES), value, jnp.int32)
    for copy in copies[:held]:
        copy.wait()
    edges = [masked(psi[s], dims[0, first + s]) for s in range(held)]
    for s in range(held):
        v0[s] = edges[s]
    low = edges[0].astype(BF16)
    high = edges[-1].astype(BF16)
    inside[0] = jnp.where(odd == 1, low, high)
    across[0] = jnp.where(odd == 1, high, low)
    for copy in copies[held:]:
        copy.wait()
    for m in range(2):
        inside[1 + m] = jnp.where(odd == 1, blocks[m], blocks[2 + m])
        across[1 + m] = jnp.where(odd == 1, blocks[2 + m], blocks[m])


def put_local(v, env, r, shift, **ready):
    facts = Facts(r["facts"])
    out = local_part(v, env, r["right"], r["outer"], r["inner"], shift, **ready)
    for s, block in enumerate(out):
        r["q"][s] = block
    if "inside" not in r:
        return
    inside, across = swapped(facts.odd, out[0], out[-1])
    r["inside"][...] = inside.astype(BF16)
    r["across"][...] = across.astype(BF16)


def local_kernel(shift, names, *refs):
    r = dict(zip(names, refs))
    arrived = refs[-1]
    copies = {}
    for n in ("outer", "inner"):
        copies[n] = pltpu.make_async_copy(r[n + "_at"], r[n], arrived.at[len(copies)])
    for n in ("right", "left"):
        for w in range(r[n].shape[1]):
            copies[n, w] = pltpu.make_async_copy(
                r[n + "_at"].at[0, w], r[n].at[0, w], arrived.at[len(copies)]
            )
    order = [("right", w) for w in range(r["right"].shape[1])] + ["outer", "inner"]
    order += [("left", w) for w in range(r["left"].shape[1])]
    for key in order:
        copies[key].start()

    def ready(*what):
        for key in ("outer", "inner") if what == ("hops",) else (what,):
            copies[key].wait()

    v = [r["v0"][s] for s in range(r["v0"].shape[0])]
    put_local(v, lambda w, s: r["left"][0, w, s], r, shift, ready=ready)
    r["dots"][...] = dot_rows([v], v)


def ghosts(k, facts, r):
    came = []
    for n, (name, row) in enumerate((("inside", facts.INSIDE), ("across", facts.ACROSS))):
        ref = r["came_" + name]
        block = (ref[0] if len(ref.shape) == 3 else ref[...]).astype(F32)
        if k > 0:
            block = block - r["given"][n]
        came.append(masked(block, facts.row(row)))
    low, high = swapped(facts.odd, *came)
    return low.astype(BF16), high.astype(BF16)


def put_given(v, facts, r):
    sent = swapped(facts.odd, v[0], v[-1])
    for n, (block, name) in enumerate(zip(sent, ("hops_inside", "hops_across"))):
        r["gives"][n] = TAU * hop(block.astype(BF16), r[name][2], r[name][1])


def step_kernel(k, shift, names, *refs):
    r = dict(zip(names, refs))
    facts = Facts(r["facts"])
    outer, inner = r["outer"], r["inner"]
    held = r["part"].shape[0]
    low, high = ghosts(k, facts, r)
    v = [r["part"][s] for s in range(held)]
    v[0] = v[0] - TAU * hop(low, inner[0, 0, 0], outer[0, 0, 0])
    v[-1] = v[-1] - TAU * hop(high, inner[0, 1, held - 1], outer[0, 1, held - 1])
    v = [masked(block, facts.dim(s)) for s, block in enumerate(v)]
    for s in range(held):
        r["v"][s] = v[s]
    basis = [[r[f"v{i}"][s] for s in range(held)] for i in range(k + 1)]
    if k + 1 < ITERS:
        put_given(basis[k], facts, r)
        left = r["left"]
        env = (lambda w, s: left[0, w, s]) if len(left.shape) == 5 else (lambda w, s: left[w, s])
        put_local(v, env, r, shift)
        r["dots"][...] = dot_rows(basis + [v], v)
    else:
        lanes = lax.broadcasted_iota(jnp.int32, (ROWS, LANES), 1)
        rows = lax.broadcasted_iota(jnp.int32, (ROWS, LANES), 0)
        line = jnp.zeros((1, LANES), F32)
        for j in range(ITERS + 1):
            part = r[f"dots{j}"][...] if j < ITERS else dot_rows(basis + [v], v)
            part = jnp.sum(part, axis=1, keepdims=True)
            line = line + jnp.sum(
                jnp.where(lanes == ROWS * j + rows, part, 0.0), axis=0, keepdims=True
            )
        for n in range(r["line"].shape[0]):
            r["line"][n] = line


def combination(line, live_count, shift):
    lanes = lax.broadcasted_iota(jnp.int32, (1, LANES), 1)
    gram = {}
    for j in range(ITERS + 1):
        for i in range(j + 1):
            gram[i, j] = jnp.sum(
                jnp.where(lanes == ROWS * j + i, line, 0.0), axis=1, keepdims=True
            )
            gram[j, i] = gram[i, j]
    coefs = [jnp.ones((1, 1), F32)]
    energy = None
    for _ in range(ITERS):
        n = len(coefs)
        onto = [sum(coefs[i] * gram[i, j] for i in range(n)) for j in range(n + 1)]
        raised = [sum(coefs[i] * gram[i + 1, j] for i in range(n)) for j in range(1, n + 1)]
        self_dot = sum(coefs[j] * onto[j] for j in range(n))
        cross = sum(coefs[j] * onto[j + 1] for j in range(n))
        square = sum(coefs[j] * raised[j] for j in range(n))
        ratio = cross / self_dot
        gain = 1.0 - ratio
        energy = shift + gain / TAU
        norm = square + gain * (2.0 * cross + gain * self_dot)
        scale = jnp.sqrt(live_count / norm)
        moved = [gain * c for c in coefs] + [jnp.zeros((1, 1), F32)]
        moved = [moved[0]] + [moved[i + 1] + coefs[i] for i in range(n)]
        coefs = [scale * c for c in moved]
    return coefs, energy


def join_kernel(shift, names, *refs):
    r = dict(zip(names, refs))
    facts = Facts(r["facts"])
    line = jnp.sum(r["lines"][...], axis=0)
    coefs, _ = combination(line, facts.row(facts.LIVE).astype(F32), shift)
    held, cap, _ = r["v0"].shape
    pad = r["factor"].shape[1] - cap
    blocks = [sum(c * r[f"v{k}"][s] for k, c in enumerate(coefs)) for s in range(held)]
    for s, block in enumerate(blocks):
        r["x"][s] = block
        r["factor"][s, :cap] = block.astype(BF16)
        dim = jnp.broadcast_to(facts.dim(s).astype(F32), (pad, cap))
        r["factor"][s, cap:] = dim.astype(BF16)
    inside, across = swapped(facts.odd, blocks[0], blocks[-1])
    r["inside"][...] = inside.astype(BF16)
    r["across"][...] = across.astype(BF16)


def grown(env, factor):
    cap = env.shape[0]
    block = factor[:cap]
    product = nn(block.T, nn(env, block).astype(BF16))
    return (product / factor[cap : cap + 1].astype(F32)).astype(BF16)


def grow_kernel(left, factor, out, token, held_out, sent):
    copies = []
    for w in range(left.shape[1]):
        for s in range(left.shape[2]):
            held_out[w, s] = grown(left[0, w, s], factor[s])
        copies.append(pltpu.make_async_copy(held_out.at[w], out.at[0, w], sent.at[w]))
        copies[-1].start()
    token[...] = jnp.zeros_like(token)
    for copy in copies:
        copy.wait()


def second_kernel(shift, names, *refs):
    r = dict(zip(names, refs))
    facts = Facts(r["facts"])
    held = r["v0"].shape[0]
    first = facts.row(facts.FIRST) == 1
    for s in range(held):
        for w in range(r["left"].shape[1]):
            new = grown(r["earlier"][0, w, s], r["factor"][s]).astype(F32)
            kept = r["left"][0, w, s].astype(F32)
            r["env"][w, s] = jnp.where(first, kept, new).astype(BF16)
    v = [r["v0"][s] for s in range(held)]
    put_local(v, lambda w, s: r["env"][w, s], r, shift)
    r["dots"][...] = dot_rows([v], v)


def finish_kernel(shift, names, *refs):
    r = dict(zip(names, refs))
    facts = Facts(r["facts"])
    line = jnp.sum(r["lines"][...], axis=0)
    coefs, energy = combination(line, facts.row(facts.LIVE).astype(F32), shift)
    for s in range(r["v0"].shape[0]):
        r["x"][0, s] = sum(c * r[f"v{k}"][s] for k, c in enumerate(coefs))
    r["energy"][0] = energy[0, 0]


def in_hbm(array):
    return pltpu.with_memory_space_constraint(array, pltpu.HBM)


def struct(shape, dtype):
    return jax.ShapeDtypeStruct(shape, dtype)


def call(kernel, name, ins, outs, flops=0, specs=None, scratch=(), outside=()):
    args = tuple(ins.values())
    values = pl.pallas_call(
        kernel,
        out_shape=tuple(outs.values()),
        in_specs=specs or [VMEM] * len(args),
        out_specs=tuple(
            SMEM if o.shape == (1,) else HBM if n in outside else VMEM for n, o in outs.items()
        ),
        scratch_shapes=scratch,
        name=name,
        compiler_params=pltpu.CompilerParams(vmem_limit_bytes=VMEM_LIMIT),
        cost_estimate=pl.CostEstimate(
            flops=flops,
            transcendentals=0,
            bytes_accessed=sum(a.size * a.dtype.itemsize for a in args),
        ),
    )(*args)
    return dict(zip(outs, values))


def body(psi, left_env, right_env, hop_outer, hop_inner, dims):
    _, terms, held, cap, _ = left_env.shape
    shift = float(terms)
    size = lax.axis_size("sec")
    place = jnp.stack([lax.axis_index("sec"), lax.axis_index("seg")]).astype(jnp.int32)
    block = struct((cap, cap), BF16)
    blocks = struct((held, cap, cap), F32)
    pair = struct((2, cap, cap), F32)
    triple = struct((3, cap, cap), BF16)
    dots_of = struct((ROWS, LANES), F32)
    local_outs = {"q": blocks, "inside": block, "across": block, "dots": dots_of}
    pairs = [(i, i ^ 1) for i in range(size)]
    others = [(i, (i + 1 if i % 2 else i - 1) % size) for i in range(size)]
    segments = lax.axis_size("seg")
    onward = [(i, (i + 1) % segments) for i in range(segments)]
    one = 2 * cap**3

    def exchange(got):
        return {
            "came_inside": lax.ppermute(got["inside"], "sec", pairs),
            "came_across": lax.ppermute(got["across"], "sec", others),
        }

    def made(kernel, name, ins, outs, flops=0, **more):
        names = tuple(ins) + tuple(outs)
        return call(functools.partial(kernel, names), name, ins, outs, flops, **more)

    start = call(
        start_kernel,
        "start",
        {
            "place": place,
            "dims": in_hbm(dims),
            "psi": in_hbm(psi),
            "outer": in_hbm(hop_outer),
            "inner": in_hbm(hop_inner),
        },
        {
            "v0": blocks,
            "inside": triple,
            "across": triple,
            "facts": struct((ROWS * (1 + (4 + held) // ROWS), LANES), jnp.int32),
        },
        specs=[SMEM, HBM, HBM, HBM, HBM],
        scratch=[
            pltpu.SMEM(dims.shape, jnp.int32),
            pltpu.VMEM((held, cap, cap), F32),
            pltpu.VMEM((4, cap, cap), BF16),
            pltpu.SemaphoreType.DMA((held + 5,)),
        ],
    )
    facts = start["facts"]
    came = exchange(start)
    hops = {"hops_inside": came["came_inside"], "hops_across": came["came_across"]}
    earlier = lax.ppermute(left_env, "seg", onward)

    def relaxed(v0, came, got, env):
        basis = {"v0": v0}
        dots = {"dots0": got["dots"]}
        for k in range(ITERS):
            ins = {"part": got["q"], **common, **basis, **came}
            if k > 0:
                ins["given"] = got["gives"]
            if k + 1 < ITERS:
                came = exchange(got)
                ins.update(left=env, **hops)
                outs = {"v": blocks, "gives": pair, **local_outs}
                if k + 2 == ITERS:
                    del outs["inside"], outs["across"]
            else:
                del ins["right"]
                ins.update(dots)
                outs = {"v": blocks, "line": struct((size, 1, LANES), F32)}
            kernel = functools.partial(step_kernel, k, shift)
            got = made(kernel, f"step{k}", ins, outs, flops=one * 36)
            basis[f"v{k + 1}"] = got["v"]
            if k + 1 < ITERS:
                dots[f"dots{k + 1}"] = got["dots"]
        return basis, lax.all_to_all(got["line"], "sec", 0, 0)

    got = made(
        functools.partial(local_kernel, shift),
        "local",
        {
            "facts": facts,
            "v0": start["v0"],
            "left_at": in_hbm(left_env),
            "right_at": in_hbm(right_env),
            "outer_at": in_hbm(hop_outer),
            "inner_at": in_hbm(hop_inner),
        },
        {
            "left": struct(left_env.shape, BF16),
            "right": struct(right_env.shape, BF16),
            "outer": struct(hop_outer.shape, BF16),
            "inner": struct(hop_inner.shape, BF16),
            **local_outs,
        },
        flops=one * 28,
        specs=[VMEM, VMEM, HBM, HBM, HBM, HBM],
        scratch=[pltpu.SemaphoreType.DMA((2 + 2 * terms,))],
    )
    left = got["left"]
    common = {"facts": facts, **{n: got[n] for n in ("outer", "inner", "right")}}
    basis, lines = relaxed(start["v0"], came, got, left)
    joined = made(
        functools.partial(join_kernel, shift),
        "join",
        {"facts": facts, "lines": lines, **basis},
        {
            "x": blocks,
            "factor": struct((held, cap + 16, cap), BF16),
            "inside": block,
            "across": block,
        },
    )
    factor = joined["factor"]
    earlier_factor = lax.ppermute(factor, "seg", onward)
    came = exchange(joined)
    renewed = call(
        grow_kernel,
        "grow",
        {"left": left, "factor": factor},
        {"out": struct(left_env.shape, BF16), "token": dots_of},
        flops=one * 24,
        scratch=[
            pltpu.VMEM((terms, held, cap, cap), BF16),
            pltpu.SemaphoreType.DMA((terms,)),
        ],
        outside=("out",),
    )
    got = made(
        functools.partial(second_kernel, shift),
        "second",
        {
            "v0": joined["x"],
            "left": left,
            "earlier": earlier,
            "factor": earlier_factor,
            "token": renewed["token"],
            **common,
        },
        {"env": struct((terms, held, cap, cap), BF16), **local_outs},
        flops=one * 52,
    )
    basis, lines = relaxed(joined["x"], came, got, got["env"])
    done = made(
        functools.partial(finish_kernel, shift),
        "finish",
        {"facts": facts, "lines": lines, **basis},
        {"x": struct(psi.shape, F32), "energy": struct((1,), F32)},
    )
    return (done["x"], done["energy"], renewed["out"])


def solution(mesh):
    return jax.shard_map(
        body,
        mesh=mesh,
        in_specs=(
            P("seg", "sec", None, None),
            P("seg", None, "sec", None, None),
            P("seg", None, "sec", None, None),
            P("seg", None, "sec", None, None),
            P("seg", None, "sec", None, None),
            P("seg", None),
        ),
        out_specs=(P("seg", "sec", None, None), P("seg"), P("seg", None, "sec", None, None)),
        check_vma=False,
    )
```

```python
import functools

import jax
import jax.numpy as jnp
from jax import lax
from jax.experimental import pallas as pl
from jax.experimental.pallas import tpu as pltpu
from jax.sharding import PartitionSpec as P

ITERS = 4
TAU = 0.05
F32 = jnp.float32
BF16 = jnp.bfloat16
LANES = 128
VMEM_LIMIT = 24 << 20
ROWS = 8

VMEM = pl.BlockSpec(memory_space=pltpu.VMEM)
SMEM = pl.BlockSpec(memory_space=pltpu.SMEM)
HBM = pl.BlockSpec(memory_space=pltpu.HBM)


def nn(a, b):
    return lax.dot_general(a, b, (((1,), (0,)), ((), ())), preferred_element_type=F32)


def nt(a, b):
    return lax.dot_general(a, b, (((1,), (1,)), ((), ())), preferred_element_type=F32)


def hop(block, inner, outer):
    return nn(outer, nt(block, inner).astype(BF16))


def masked(block, dim):
    rows = lax.broadcasted_iota(jnp.int32, block.shape, 0)
    cols = lax.broadcasted_iota(jnp.int32, block.shape, 1)
    return jnp.where(jnp.logical_and(rows < dim, cols < dim), block, 0.0)


def local_part(v, env, right, outer, inner, shift, ready=lambda *what: None):
    held = len(v)
    terms = right.shape[1]
    b = [x.astype(BF16) for x in v]
    half = []
    for w in range(terms):
        ready("right", w)
        half.append([nt(b[s], right[0, w, s]).astype(BF16) for s in range(held)])
    image = [None] * held
    ready("hops")
    for s in range(held):
        if s > 0:
            image[s] = hop(b[s - 1], inner[0, 0, s], outer[0, 0, s])
        if s + 1 < held:
            above = hop(b[s + 1], inner[0, 1, s], outer[0, 1, s])
            image[s] = above if image[s] is None else image[s] + above
    for w in range(terms):
        ready("left", w)
        for s in range(held):
            term = nn(env(w, s), half[w][s])
            image[s] = term if image[s] is None else image[s] + term
    return [v[s] * (1.0 + TAU * shift) - TAU * image[s] for s in range(held)]


def dot_rows(basis, last):
    rows = lax.broadcasted_iota(jnp.int32, (ROWS, LANES), 0)
    out = jnp.zeros((ROWS, LANES), F32)
    for i, other in enumerate(basis):
        total = sum(jnp.sum(a * b, axis=0, keepdims=True) for a, b in zip(other, last))
        total = sum(total[:, n : n + LANES] for n in range(0, total.shape[1], LANES))
        out = jnp.where(rows == i, total, out)
    return out


class Facts:
    ODD, FIRST, LIVE, INSIDE, ACROSS, DIM = range(6)

    def __init__(self, ref):
        self.ref = ref

    def row(self, n):
        return self.ref[n : n + 1, 0:1]

    @property
    def odd(self):
        return self.row(self.ODD) == 1

    def dim(self, s):
        return self.row(self.DIM + s)


def swapped(odd, low, high):
    return jnp.where(odd, low, high), jnp.where(odd, high, low)


def start_kernel(
    place, dims_at, psi_at, outer_at, inner_at, v0, inside, across, facts, dims, psi, blocks, arrived
):
    held, cap, _ = psi.shape
    known = pltpu.make_async_copy(dims_at, dims, arrived.at[held + 4])
    known.start()
    copies = [pltpu.make_async_copy(psi_at.at[0, s], psi.at[s], arrived.at[s]) for s in range(held)]
    for n, (side, s) in enumerate(((0, 0), (1, held - 1))):
        for m, array in enumerate((outer_at, inner_at)):
            copies.append(
                pltpu.make_async_copy(
                    array.at[0, side, s], blocks.at[2 * n + m], arrived.at[held + 2 * n + m]
                )
            )
    for copy in copies:
        copy.start()
    known.wait()
    first = place[0] * held
    last = dims.shape[1] - 1
    odd = place[0] % 2
    low_dim = jnp.where(first == 0, 0, dims[0, jnp.maximum(first - 1, 0)])
    high_dim = jnp.where(first + held > last, 0, dims[0, jnp.minimum(first + held, last)])
    live = jnp.int32(0)
    for s in range(dims.shape[1]):
        live = live + dims[0, s] * dims[0, s]
    rows = [
        odd,
        jnp.where(place[1] == 0, 1, 0),
        live,
        jnp.where(odd == 1, low_dim, high_dim),
        jnp.where(odd == 1, high_dim, low_dim),
    ] + [dims[0, first + s] for s in range(held)]
    for n, value in enumerate(rows):
        facts[n : n + 1, :] = jnp.full((1, LANES), value, jnp.int32)
    for copy in copies[:held]:
        copy.wait()
    edges = [masked(psi[s], dims[0, first + s]) for s in range(held)]
    for s in range(held):
        v0[s] = edges[s]
    low = edges[0].astype(BF16)
    high = edges[-1].astype(BF16)
    inside[0] = jnp.where(odd == 1, low, high)
    across[0] = jnp.where(odd == 1, high, low)
    for copy in copies[held:]:
        copy.wait()
    for m in range(2):
        inside[1 + m] = jnp.where(odd == 1, blocks[m], blocks[2 + m])
        across[1 + m] = jnp.where(odd == 1, blocks[2 + m], blocks[m])


def put_local(v, env, r, shift, **ready):
    facts = Facts(r["facts"])
    out = local_part(v, env, r["right"], r["outer"], r["inner"], shift, **ready)
    for s, block in enumerate(out):
        r["q"][s] = block
    if "inside" not in r:
        return
    inside, across = swapped(facts.odd, out[0], out[-1])
    r["inside"][...] = inside.astype(BF16)
    r["across"][...] = across.astype(BF16)


def local_kernel(shift, names, *refs):
    r = dict(zip(names, refs))
    arrived = refs[-1]
    copies = {}
    for n in ("outer", "inner"):
        copies[n] = pltpu.make_async_copy(r[n + "_at"], r[n], arrived.at[len(copies)])
    for n in ("right", "left"):
        for w in range(r[n].shape[1]):
            copies[n, w] = pltpu.make_async_copy(
                r[n + "_at"].at[0, w], r[n].at[0, w], arrived.at[len(copies)]
            )
    order = [("right", w) for w in range(r["right"].shape[1])] + ["outer", "inner"]
    order += [("left", w) for w in range(r["left"].shape[1])]
    for key in order:
        copies[key].start()

    def ready(*what):
        for key in ("outer", "inner") if what == ("hops",) else (what,):
            copies[key].wait()

    v = [r["v0"][s] for s in range(r["v0"].shape[0])]
    put_local(v, lambda w, s: r["left"][0, w, s], r, shift, ready=ready)


def ghosts(k, facts, r):
    came = []
    for n, (name, row) in enumerate((("inside", facts.INSIDE), ("across", facts.ACROSS))):
        ref = r["came_" + name]
        block = (ref[0] if len(ref.shape) == 3 else ref[...]).astype(F32)
        if k > 0:
            block = block - r["given"][n]
        came.append(masked(block, facts.row(row)))
    low, high = swapped(facts.odd, *came)
    return low.astype(BF16), high.astype(BF16)


def put_given(v, facts, r):
    sent = swapped(facts.odd, v[0], v[-1])
    for n, (block, name) in enumerate(zip(sent, ("hops_inside", "hops_across"))):
        r["gives"][n] = TAU * hop(block.astype(BF16), r[name][2], r[name][1])


def step_kernel(k, shift, names, *refs):
    r = dict(zip(names, refs))
    facts = Facts(r["facts"])
    outer, inner = r["outer"], r["inner"]
    held = r["part"].shape[0]
    low, high = ghosts(k, facts, r)
    v = [r["part"][s] for s in range(held)]
    v[0] = v[0] - TAU * hop(low, inner[0, 0, 0], outer[0, 0, 0])
    v[-1] = v[-1] - TAU * hop(high, inner[0, 1, held - 1], outer[0, 1, held - 1])
    v = [masked(block, facts.dim(s)) for s, block in enumerate(v)]
    for s in range(held):
        r["v"][s] = v[s]
    basis = [[r[f"v{i}"][s] for s in range(held)] for i in range(k + 1)]
    if k + 1 < ITERS:
        put_given(basis[k], facts, r)
        left = r["left"]
        env = (lambda w, s: left[0, w, s]) if len(left.shape) == 5 else (lambda w, s: left[w, s])
        put_local(v, env, r, shift)
        if "dots" in r:
            basis = basis + [v]
            for j in range(k + 2):
                r["dots"][j] = dot_rows(basis[: j + 1], basis[j])
    else:
        lanes = lax.broadcasted_iota(jnp.int32, (ROWS, LANES), 1)
        rows = lax.broadcasted_iota(jnp.int32, (ROWS, LANES), 0)
        line = jnp.zeros((1, LANES), F32)
        for j in range(ITERS + 1):
            part = r["dots_before"][j] if j < ITERS else dot_rows(basis + [v], v)
            part = jnp.sum(part, axis=1, keepdims=True)
            line = line + jnp.sum(
                jnp.where(lanes == ROWS * j + rows, part, 0.0), axis=0, keepdims=True
            )
        for n in range(r["line"].shape[0]):
            r["line"][n] = line


def combination(line, live_count, shift):
    lanes = lax.broadcasted_iota(jnp.int32, (1, LANES), 1)
    gram = {}
    for j in range(ITERS + 1):
        for i in range(j + 1):
            gram[i, j] = jnp.sum(
                jnp.where(lanes == ROWS * j + i, line, 0.0), axis=1, keepdims=True
            )
            gram[j, i] = gram[i, j]
    coefs = [jnp.ones((1, 1), F32)]
    energy = None
    for _ in range(ITERS):
        n = len(coefs)
        onto = [sum(coefs[i] * gram[i, j] for i in range(n)) for j in range(n + 1)]
        raised = [sum(coefs[i] * gram[i + 1, j] for i in range(n)) for j in range(1, n + 1)]
        self_dot = sum(coefs[j] * onto[j] for j in range(n))
        cross = sum(coefs[j] * onto[j + 1] for j in range(n))
        square = sum(coefs[j] * raised[j] for j in range(n))
        ratio = cross / self_dot
        gain = 1.0 - ratio
        energy = shift + gain / TAU
        norm = square + gain * (2.0 * cross + gain * self_dot)
        scale = jnp.sqrt(live_count / norm)
        moved = [gain * c for c in coefs] + [jnp.zeros((1, 1), F32)]
        moved = [moved[0]] + [moved[i + 1] + coefs[i] for i in range(n)]
        coefs = [scale * c for c in moved]
    return coefs, energy


def join_kernel(shift, names, *refs):
    r = dict(zip(names, refs))
    facts = Facts(r["facts"])
    line = jnp.sum(r["lines"][...], axis=0)
    coefs, _ = combination(line, facts.row(facts.LIVE).astype(F32), shift)
    held, cap, _ = r["v0"].shape
    pad = r["factor"].shape[1] - cap
    blocks = [sum(c * r[f"v{k}"][s] for k, c in enumerate(coefs)) for s in range(held)]
    for s, block in enumerate(blocks):
        r["x"][s] = block
        r["factor"][s, :cap] = block.astype(BF16)
        dim = jnp.broadcast_to(facts.dim(s).astype(F32), (pad, cap))
        r["factor"][s, cap:] = dim.astype(BF16)
    inside, across = swapped(facts.odd, blocks[0], blocks[-1])
    r["inside"][...] = inside.astype(BF16)
    r["across"][...] = across.astype(BF16)


def grown(env, factor):
    cap = env.shape[0]
    block = factor[:cap]
    product = nn(block.T, nn(env, block).astype(BF16))
    return (product / factor[cap : cap + 1].astype(F32)).astype(BF16)


def grow_kernel(left, factor, out, token, held_out, sent):
    copies = []
    for w in range(left.shape[1]):
        for s in range(left.shape[2]):
            held_out[w, s] = grown(left[0, w, s], factor[s])
        copies.append(pltpu.make_async_copy(held_out.at[w], out.at[0, w], sent.at[w]))
        copies[-1].start()
    token[...] = jnp.zeros_like(token)
    for copy in copies:
        copy.wait()


def second_kernel(shift, names, *refs):
    r = dict(zip(names, refs))
    facts = Facts(r["facts"])
    held = r["v0"].shape[0]
    first = facts.row(facts.FIRST) == 1
    for s in range(held):
        for w in range(r["left"].shape[1]):
            new = grown(r["earlier"][0, w, s], r["factor"][s]).astype(F32)
            kept = r["left"][0, w, s].astype(F32)
            r["env"][w, s] = jnp.where(first, kept, new).astype(BF16)
    v = [r["v0"][s] for s in range(held)]
    put_local(v, lambda w, s: r["env"][w, s], r, shift)


def finish_kernel(shift, names, *refs):
    r = dict(zip(names, refs))
    facts = Facts(r["facts"])
    line = jnp.sum(r["lines"][...], axis=0)
    coefs, energy = combination(line, facts.row(facts.LIVE).astype(F32), shift)
    for s in range(r["v0"].shape[0]):
        r["x"][0, s] = sum(c * r[f"v{k}"][s] for k, c in enumerate(coefs))
    r["energy"][0] = energy[0, 0]


def in_hbm(array):
    return pltpu.with_memory_space_constraint(array, pltpu.HBM)


def struct(shape, dtype):
    return jax.ShapeDtypeStruct(shape, dtype)


def call(kernel, name, ins, outs, flops=0, specs=None, scratch=(), outside=()):
    args = tuple(ins.values())
    values = pl.pallas_call(
        kernel,
        out_shape=tuple(outs.values()),
        in_specs=specs or [VMEM] * len(args),
        out_specs=tuple(
            SMEM if o.shape == (1,) else HBM if n in outside else VMEM for n, o in outs.items()
        ),
        scratch_shapes=scratch,
        name=name,
        compiler_params=pltpu.CompilerParams(vmem_limit_bytes=VMEM_LIMIT),
        cost_estimate=pl.CostEstimate(
            flops=flops,
            transcendentals=0,
            bytes_accessed=sum(a.size * a.dtype.itemsize for a in args),
        ),
    )(*args)
    return dict(zip(outs, values))


def body(psi, left_env, right_env, hop_outer, hop_inner, dims):
    _, terms, held, cap, _ = left_env.shape
    shift = float(terms)
    size = lax.axis_size("sec")
    place = jnp.stack([lax.axis_index("sec"), lax.axis_index("seg")]).astype(jnp.int32)
    block = struct((cap, cap), BF16)
    blocks = struct((held, cap, cap), F32)
    pair = struct((2, cap, cap), F32)
    triple = struct((3, cap, cap), BF16)
    token = struct((ROWS, LANES), F32)
    local_outs = {"q": blocks, "inside": block, "across": block}
    pairs = [(i, i ^ 1) for i in range(size)]
    others = [(i, (i + 1 if i % 2 else i - 1) % size) for i in range(size)]
    segments = lax.axis_size("seg")
    onward = [(i, (i + 1) % segments) for i in range(segments)]
    one = 2 * cap**3

    def exchange(got):
        return {
            "came_across": lax.ppermute(got["across"], "sec", others),
            "came_inside": lax.ppermute(got["inside"], "sec", pairs),
        }

    def made(kernel, name, ins, outs, flops=0, **more):
        names = tuple(ins) + tuple(outs)
        return call(functools.partial(kernel, names), name, ins, outs, flops, **more)

    start = call(
        start_kernel,
        "start",
        {
            "place": place,
            "dims": in_hbm(dims),
            "psi": in_hbm(psi),
            "outer": in_hbm(hop_outer),
            "inner": in_hbm(hop_inner),
        },
        {
            "v0": blocks,
            "inside": triple,
            "across": triple,
            "facts": struct((ROWS * (1 + (4 + held) // ROWS), LANES), jnp.int32),
        },
        specs=[SMEM, HBM, HBM, HBM, HBM],
        scratch=[
            pltpu.SMEM(dims.shape, jnp.int32),
            pltpu.VMEM((held, cap, cap), F32),
            pltpu.VMEM((4, cap, cap), BF16),
            pltpu.SemaphoreType.DMA((held + 5,)),
        ],
    )
    facts = start["facts"]
    came = exchange(start)
    hops = {"hops_inside": came["came_inside"], "hops_across": came["came_across"]}
    earlier = lax.ppermute(left_env, "seg", onward)

    def relaxed(v0, came, got, env):
        basis = {"v0": v0}
        for k in range(ITERS):
            ins = {"part": got["q"], **common, **basis, **came}
            if k > 0:
                ins["given"] = got["gives"]
            if k + 1 < ITERS:
                came = exchange(got)
                ins.update(left=env, **hops)
                outs = {"v": blocks, "gives": pair, **local_outs}
                if k + 2 == ITERS:
                    del outs["inside"], outs["across"]
                    outs["dots"] = struct((ITERS, ROWS, LANES), F32)
            else:
                del ins["right"]
                ins["dots_before"] = got["dots"]
                outs = {"v": blocks, "line": struct((size, 1, LANES), F32)}
            kernel = functools.partial(step_kernel, k, shift)
            got = made(kernel, f"step{k}", ins, outs, flops=one * 36)
            basis[f"v{k + 1}"] = got["v"]
        return basis, lax.all_to_all(got["line"], "sec", 0, 0)

    got = made(
        functools.partial(local_kernel, shift),
        "local",
        {
            "facts": facts,
            "v0": start["v0"],
            "left_at": in_hbm(left_env),
            "right_at": in_hbm(right_env),
            "outer_at": in_hbm(hop_outer),
            "inner_at": in_hbm(hop_inner),
        },
        {
            "left": struct(left_env.shape, BF16),
            "right": struct(right_env.shape, BF16),
            "outer": struct(hop_outer.shape, BF16),
            "inner": struct(hop_inner.shape, BF16),
            **local_outs,
        },
        flops=one * 28,
        specs=[VMEM, VMEM, HBM, HBM, HBM, HBM],
        scratch=[pltpu.SemaphoreType.DMA((2 + 2 * terms,))],
    )
    left = got["left"]
    common = {"facts": facts, **{n: got[n] for n in ("outer", "inner", "right")}}
    basis, lines = relaxed(start["v0"], came, got, left)
    joined = made(
        functools.partial(join_kernel, shift),
        "join",
        {"facts": facts, "lines": lines, **basis},
        {
            "x": blocks,
            "factor": struct((held, cap + 16, cap), BF16),
            "inside": block,
            "across": block,
        },
    )
    factor = joined["factor"]
    earlier_factor = lax.ppermute(factor, "seg", onward)
    came = exchange(joined)
    renewed = call(
        grow_kernel,
        "grow",
        {"left": left, "factor": factor},
        {"out": struct(left_env.shape, BF16), "token": token},
        flops=one * 24,
        scratch=[
            pltpu.VMEM((terms, held, cap, cap), BF16),
            pltpu.SemaphoreType.DMA((terms,)),
        ],
        outside=("out",),
    )
    got = made(
        functools.partial(second_kernel, shift),
        "second",
        {
            "v0": joined["x"],
            "left": left,
            "earlier": earlier,
            "factor": earlier_factor,
            "token": renewed["token"],
            **common,
        },
        {"env": struct((terms, held, cap, cap), BF16), **local_outs},
        flops=one * 52,
    )
    basis, lines = relaxed(joined["x"], came, got, got["env"])
    done = made(
        functools.partial(finish_kernel, shift),
        "finish",
        {"facts": facts, "lines": lines, **basis},
        {"x": struct(psi.shape, F32), "energy": struct((1,), F32)},
    )
    return (done["x"], done["energy"], renewed["out"])


def solution(mesh):
    return jax.shard_map(
        body,
        mesh=mesh,
        in_specs=(
            P("seg", "sec", None, None),
            P("seg", None, "sec", None, None),
            P("seg", None, "sec", None, None),
            P("seg", None, "sec", None, None),
            P("seg", None, "sec", None, None),
            P("seg", None),
        ),
        out_specs=(P("seg", "sec", None, None), P("seg"), P("seg", None, "sec", None, None)),
        check_vma=False,
    )
```

```python
import functools

import jax
import jax.numpy as jnp
from jax import lax
from jax.experimental import pallas as pl
from jax.experimental.pallas import tpu as pltpu
from jax.sharding import PartitionSpec as P


ITERS = 4
TAU = 0.05
F32 = jnp.float32
BF16 = jnp.bfloat16
LANES = 128
VMEM_LIMIT = 24 << 20
ROWS = 8

VMEM = pl.BlockSpec(memory_space=pltpu.VMEM)
SMEM = pl.BlockSpec(memory_space=pltpu.SMEM)
HBM = pl.BlockSpec(memory_space=pltpu.HBM)


def nn(a, b):
    return lax.dot_general(a, b, (((1,), (0,)), ((), ())), preferred_element_type=F32)


def nt(a, b):
    return lax.dot_general(a, b, (((1,), (1,)), ((), ())), preferred_element_type=F32)


def hop(block, inner, outer):
    return nn(outer, nt(block, inner).astype(BF16))


def masked(block, dim):
    rows = lax.broadcasted_iota(jnp.int32, block.shape, 0)
    cols = lax.broadcasted_iota(jnp.int32, block.shape, 1)
    return jnp.where(jnp.logical_and(rows < dim, cols < dim), block, 0.0)


def local_part(v, env, right, outer, inner, shift, ready=lambda *what: None):
    held = len(v)
    terms = right.shape[1]
    b = [x.astype(BF16) for x in v]
    half = []
    for w in range(terms):
        ready("right", w)
        half.append([nt(b[s], right[0, w, s]).astype(BF16) for s in range(held)])
    image = [None] * held
    ready("hops")
    for s in range(held):
        if s > 0:
            image[s] = hop(b[s - 1], inner[0, 0, s], outer[0, 0, s])
        if s + 1 < held:
            above = hop(b[s + 1], inner[0, 1, s], outer[0, 1, s])
            image[s] = above if image[s] is None else image[s] + above
    for w in range(terms):
        ready("left", w)
        for s in range(held):
            term = nn(env(w, s), half[w][s])
            image[s] = term if image[s] is None else image[s] + term
    return [v[s] * (1.0 + TAU * shift) - TAU * image[s] for s in range(held)]


def dot_rows(basis, last):
    rows = lax.broadcasted_iota(jnp.int32, (ROWS, LANES), 0)
    out = jnp.zeros((ROWS, LANES), F32)
    for i, other in enumerate(basis):
        total = sum(jnp.sum(a * b, axis=0, keepdims=True) for a, b in zip(other, last))
        total = sum(total[:, n : n + LANES] for n in range(0, total.shape[1], LANES))
        out = jnp.where(rows == i, total, out)
    return out


class Facts:
    ODD, FIRST, LIVE, INSIDE, ACROSS, DIM = range(6)

    def __init__(self, ref):
        self.ref = ref

    def row(self, n):
        return self.ref[n : n + 1, 0:1]

    @property
    def odd(self):
        return self.row(self.ODD) == 1

    def dim(self, s):
        return self.row(self.DIM + s)


def swapped(odd, low, high):
    return jnp.where(odd, low, high), jnp.where(odd, high, low)


def start_kernel(
    place, dims_at, psi_at, outer_at, inner_at, v0, inside, across, to_inside, to_across, facts, dims, psi, blocks, arrived
):
    held, cap, _ = psi.shape
    known = pltpu.make_async_copy(dims_at, dims, arrived.at[held + 4])
    known.start()
    copies = [pltpu.make_async_copy(psi_at.at[0, s], psi.at[s], arrived.at[s]) for s in range(held)]
    for n, (side, s) in enumerate(((0, 0), (1, held - 1))):
        for m, array in enumerate((outer_at, inner_at)):
            copies.append(
                pltpu.make_async_copy(
                    array.at[0, side, s], blocks.at[2 * n + m], arrived.at[held + 2 * n + m]
                )
            )
    for copy in copies:
        copy.start()
    known.wait()
    first = place[0] * held
    last = dims.shape[1] - 1
    odd = place[0] % 2
    low_dim = jnp.where(first == 0, 0, dims[0, jnp.maximum(first - 1, 0)])
    high_dim = jnp.where(first + held > last, 0, dims[0, jnp.minimum(first + held, last)])
    live = jnp.int32(0)
    for s in range(dims.shape[1]):
        live = live + dims[0, s] * dims[0, s]
    rows = [
        odd,
        jnp.where(place[1] == 0, 1, 0),
        live,
        jnp.where(odd == 1, low_dim, high_dim),
        jnp.where(odd == 1, high_dim, low_dim),
    ] + [dims[0, first + s] for s in range(held)]
    for n, value in enumerate(rows):
        facts[n : n + 1, :] = jnp.full((1, LANES), value, jnp.int32)
    for copy in copies[:held]:
        copy.wait()
    edges = [masked(psi[s], dims[0, first + s]) for s in range(held)]
    for s in range(held):
        v0[s] = edges[s]
    low = edges[0].astype(BF16)
    high = edges[-1].astype(BF16)
    inside[...] = jnp.where(odd == 1, low, high)
    across[...] = jnp.where(odd == 1, high, low)
    for copy in copies[held:]:
        copy.wait()
    for m in range(2):
        to_inside[m] = jnp.where(odd == 1, blocks[m], blocks[2 + m])
        to_across[m] = jnp.where(odd == 1, blocks[2 + m], blocks[m])


def put_local(v, env, r, shift, **ready):
    facts = Facts(r["facts"])
    out = local_part(v, env, r["right"], r["outer"], r["inner"], shift, **ready)
    for s, block in enumerate(out):
        r["q"][s] = block
    if "inside" not in r:
        return
    inside, across = swapped(facts.odd, out[0], out[-1])
    r["inside"][...] = inside.astype(BF16)
    r["across"][...] = across.astype(BF16)


def local_kernel(shift, names, *refs):
    r = dict(zip(names, refs))
    arrived = refs[-1]
    copies = {}
    for n in ("outer", "inner"):
        copies[n] = pltpu.make_async_copy(r[n + "_at"], r[n], arrived.at[len(copies)])
    for n in ("right", "left"):
        for w in range(r[n].shape[1]):
            copies[n, w] = pltpu.make_async_copy(
                r[n + "_at"].at[0, w], r[n].at[0, w], arrived.at[len(copies)]
            )
    order = [("right", w) for w in range(r["right"].shape[1])] + ["outer", "inner"]
    order += [("left", w) for w in range(r["left"].shape[1])]
    for key in order:
        copies[key].start()

    def ready(*what):
        for key in ("outer", "inner") if what == ("hops",) else (what,):
            copies[key].wait()

    v = [r["v0"][s] for s in range(r["v0"].shape[0])]
    put_local(v, lambda w, s: r["left"][0, w, s], r, shift, ready=ready)


def ghosts(k, facts, r):
    came = []
    if k > 0:
        before = r[f"v{k - 1}"]
        given = r["given"] if "given" in r else given_by(before, facts, r)
    for n, (name, row) in enumerate((("inside", facts.INSIDE), ("across", facts.ACROSS))):
        block = r["came_" + name][...].astype(F32)
        if k > 0:
            block = block - given[n]
        came.append(masked(block, facts.row(row)))
    low, high = swapped(facts.odd, *came)
    return low.astype(BF16), high.astype(BF16)


def given_by(v, facts, r):
    sent = swapped(facts.odd, v[0], v[held_in(v) - 1])
    return [
        TAU * hop(block.astype(BF16), r[name][1], r[name][0])
        for block, name in zip(sent, ("hops_inside", "hops_across"))
    ]


def held_in(v):
    return len(v) if isinstance(v, list) else v.shape[0]


def step_kernel(k, shift, names, *refs):
    r = dict(zip(names, refs))
    facts = Facts(r["facts"])
    outer, inner = r["outer"], r["inner"]
    held = r["part"].shape[0]
    low, high = ghosts(k, facts, r)
    v = [r["part"][s] for s in range(held)]
    v[0] = v[0] - TAU * hop(low, inner[0, 0, 0], outer[0, 0, 0])
    v[-1] = v[-1] - TAU * hop(high, inner[0, 1, held - 1], outer[0, 1, held - 1])
    v = [masked(block, facts.dim(s)) for s, block in enumerate(v)]
    for s in range(held):
        r["v"][s] = v[s]
    basis = [[r[f"v{i}"][s] for s in range(held)] for i in range(k + 1)]
    if k + 1 < ITERS:
        if "gives" in r:
            for n, block in enumerate(given_by(basis[k], facts, r)):
                r["gives"][n] = block
        left = r["left"]
        env = (lambda w, s: left[0, w, s]) if len(left.shape) == 5 else (lambda w, s: left[w, s])
        put_local(v, env, r, shift)
        if "dots" in r:
            basis = basis + [v]
            for j in range(k + 2):
                r["dots"][j] = dot_rows(basis[: j + 1], basis[j])
    else:
        lanes = lax.broadcasted_iota(jnp.int32, (ROWS, LANES), 1)
        rows = lax.broadcasted_iota(jnp.int32, (ROWS, LANES), 0)
        line = jnp.zeros((1, LANES), F32)
        for j in range(ITERS + 1):
            part = r["dots_before"][j] if j < ITERS else dot_rows(basis + [v], v)
            part = jnp.sum(part, axis=1, keepdims=True)
            line = line + jnp.sum(
                jnp.where(lanes == ROWS * j + rows, part, 0.0), axis=0, keepdims=True
            )
        for n in range(r["line"].shape[0]):
            r["line"][n] = line


def combination(line, live_count, shift):
    lanes = lax.broadcasted_iota(jnp.int32, (1, LANES), 1)
    gram = {}
    for j in range(ITERS + 1):
        for i in range(j + 1):
            gram[i, j] = jnp.sum(
                jnp.where(lanes == ROWS * j + i, line, 0.0), axis=1, keepdims=True
            )
            gram[j, i] = gram[i, j]
    coefs = [jnp.ones((1, 1), F32)]
    energy = None
    for _ in range(ITERS):
        n = len(coefs)
        onto = [sum(coefs[i] * gram[i, j] for i in range(n)) for j in range(n + 1)]
        raised = [sum(coefs[i] * gram[i + 1, j] for i in range(n)) for j in range(1, n + 1)]
        self_dot = sum(coefs[j] * onto[j] for j in range(n))
        cross = sum(coefs[j] * onto[j + 1] for j in range(n))
        square = sum(coefs[j] * raised[j] for j in range(n))
        ratio = cross / self_dot
        gain = 1.0 - ratio
        energy = shift + gain / TAU
        norm = square + gain * (2.0 * cross + gain * self_dot)
        scale = jnp.sqrt(live_count / norm)
        moved = [gain * c for c in coefs] + [jnp.zeros((1, 1), F32)]
        moved = [moved[0]] + [moved[i + 1] + coefs[i] for i in range(n)]
        coefs = [scale * c for c in moved]
    return coefs, energy


def join_kernel(shift, names, *refs):
    r = dict(zip(names, refs))
    facts = Facts(r["facts"])
    line = jnp.sum(r["lines"][...], axis=0)
    coefs, _ = combination(line, facts.row(facts.LIVE).astype(F32), shift)
    held, cap, _ = r["v0"].shape
    pad = r["factor"].shape[1] - cap
    blocks = [sum(c * r[f"v{k}"][s] for k, c in enumerate(coefs)) for s in range(held)]
    for s, block in enumerate(blocks):
        r["x"][s] = block
        r["factor"][s, :cap] = block.astype(BF16)
        dim = jnp.broadcast_to(facts.dim(s).astype(F32), (pad, cap))
        r["factor"][s, cap:] = dim.astype(BF16)
    inside, across = swapped(facts.odd, blocks[0], blocks[-1])
    r["inside"][...] = inside.astype(BF16)
    r["across"][...] = across.astype(BF16)


def grown(env, factor):
    cap = env.shape[0]
    block = factor[:cap]
    product = nn(block.T, nn(env, block).astype(BF16))
    return (product / factor[cap : cap + 1].astype(F32)).astype(BF16)


def grow_kernel(left, factor, out, token, held_out, sent):
    copies = []
    for w in range(left.shape[1]):
        for s in range(left.shape[2]):
            held_out[w, s] = grown(left[0, w, s], factor[s])
        copies.append(pltpu.make_async_copy(held_out.at[w], out.at[0, w], sent.at[w]))
        copies[-1].start()
    token[...] = jnp.zeros_like(token)
    for copy in copies:
        copy.wait()


def second_kernel(shift, names, *refs):
    r = dict(zip(names, refs))
    facts = Facts(r["facts"])
    held = r["v0"].shape[0]
    first = facts.row(facts.FIRST) == 1
    for s in range(held):
        for w in range(r["left"].shape[1]):
            new = grown(r["earlier"][0, w, s], r["factor"][s]).astype(F32)
            kept = r["left"][0, w, s].astype(F32)
            r["env"][w, s] = jnp.where(first, kept, new).astype(BF16)
    v = [r["v0"][s] for s in range(held)]
    put_local(v, lambda w, s: r["env"][w, s], r, shift)


def finish_kernel(shift, names, *refs):
    r = dict(zip(names, refs))
    facts = Facts(r["facts"])
    line = jnp.sum(r["lines"][...], axis=0)
    coefs, energy = combination(line, facts.row(facts.LIVE).astype(F32), shift)
    for s in range(r["v0"].shape[0]):
        r["x"][0, s] = sum(c * r[f"v{k}"][s] for k, c in enumerate(coefs))
    r["energy"][0] = energy[0, 0]


def in_hbm(array):
    return pltpu.with_memory_space_constraint(array, pltpu.HBM)


def struct(shape, dtype):
    return jax.ShapeDtypeStruct(shape, dtype)


def call(kernel, name, ins, outs, flops=0, specs=None, scratch=(), outside=()):
    args = tuple(ins.values())
    values = pl.pallas_call(
        kernel,
        out_shape=tuple(outs.values()),
        in_specs=specs or [VMEM] * len(args),
        out_specs=tuple(
            SMEM if o.shape == (1,) else HBM if n in outside else VMEM for n, o in outs.items()
        ),
        scratch_shapes=scratch,
        name=name,
        compiler_params=pltpu.CompilerParams(vmem_limit_bytes=VMEM_LIMIT),
        cost_estimate=pl.CostEstimate(
            flops=flops,
            transcendentals=0,
            bytes_accessed=sum(a.size * a.dtype.itemsize for a in args),
        ),
    )(*args)
    return dict(zip(outs, values))


def body(psi, left_env, right_env, hop_outer, hop_inner, dims):
    _, terms, held, cap, _ = left_env.shape
    shift = float(terms)
    size = lax.axis_size("sec")
    place = jnp.stack([lax.axis_index("sec"), lax.axis_index("seg")]).astype(jnp.int32)
    block = struct((cap, cap), BF16)
    blocks = struct((held, cap, cap), F32)
    pair = struct((2, cap, cap), F32)
    pair_of = struct((2, cap, cap), BF16)
    token = struct((ROWS, LANES), F32)
    local_outs = {"q": blocks, "inside": block, "across": block}
    pairs = [(i, i ^ 1) for i in range(size)]
    others = [(i, (i + 1 if i % 2 else i - 1) % size) for i in range(size)]
    segments = lax.axis_size("seg")
    onward = [(i, (i + 1) % segments) for i in range(segments)]
    one = 2 * cap**3

    def exchange(got):
        return {
            "came_across": lax.ppermute(got["across"], "sec", others),
            "came_inside": lax.ppermute(got["inside"], "sec", pairs),
        }

    def made(kernel, name, ins, outs, flops=0, **more):
        names = tuple(ins) + tuple(outs)
        return call(functools.partial(kernel, names), name, ins, outs, flops, **more)

    start = call(
        start_kernel,
        "start",
        {
            "place": place,
            "dims": in_hbm(dims),
            "psi": in_hbm(psi),
            "outer": in_hbm(hop_outer),
            "inner": in_hbm(hop_inner),
        },
        {
            "v0": blocks,
            "inside": block,
            "across": block,
            "to_inside": pair_of,
            "to_across": pair_of,
            "facts": struct((ROWS * (1 + (4 + held) // ROWS), LANES), jnp.int32),
        },
        specs=[SMEM, HBM, HBM, HBM, HBM],
        scratch=[
            pltpu.SMEM(dims.shape, jnp.int32),
            pltpu.VMEM((held, cap, cap), F32),
            pltpu.VMEM((4, cap, cap), BF16),
            pltpu.SemaphoreType.DMA((held + 5,)),
        ],
    )
    facts = start["facts"]
    came = exchange(start)
    sent = exchange({"inside": start["to_inside"], "across": start["to_across"]})
    hops = {"hops_inside": sent["came_inside"], "hops_across": sent["came_across"]}
    earlier = lax.ppermute(left_env, "seg", onward)

    def relaxed(v0, came, got, env, late):
        basis = {"v0": v0}
        for k in range(ITERS):
            ins = {"part": got["q"], **common, **basis, **came}
            if "gives" in got:
                ins["given"] = got["gives"]
            if k + 1 < ITERS:
                came = exchange(got)
                ins.update(left=env)
                outs = {"v": blocks, **local_outs}
                if k > 0 or not late:
                    ins.update(hops)
                    outs["gives"] = pair
                if k + 2 == ITERS:
                    del outs["inside"], outs["across"]
                    outs["dots"] = struct((ITERS, ROWS, LANES), F32)
            else:
                del ins["right"]
                ins["dots_before"] = got["dots"]
                outs = {"v": blocks, "line": struct((size, 1, LANES), F32)}
            kernel = functools.partial(step_kernel, k, shift)
            got = made(kernel, f"step{k}", ins, outs, flops=one * 36)
            basis[f"v{k + 1}"] = got["v"]
        return basis, lax.all_to_all(got["line"], "sec", 0, 0)

    got = made(
        functools.partial(local_kernel, shift),
        "local",
        {
            "facts": facts,
            "v0": start["v0"],
            "left_at": in_hbm(left_env),
            "right_at": in_hbm(right_env),
            "outer_at": in_hbm(hop_outer),
            "inner_at": in_hbm(hop_inner),
        },
        {
            "left": struct(left_env.shape, BF16),
            "right": struct(right_env.shape, BF16),
            "outer": struct(hop_outer.shape, BF16),
            "inner": struct(hop_inner.shape, BF16),
            **local_outs,
        },
        flops=one * 28,
        specs=[VMEM, VMEM, HBM, HBM, HBM, HBM],
        scratch=[pltpu.SemaphoreType.DMA((2 + 2 * terms,))],
    )
    left = got["left"]
    common = {"facts": facts, **{n: got[n] for n in ("outer", "inner", "right")}}
    basis, lines = relaxed(start["v0"], came, got, left, True)
    joined = made(
        functools.partial(join_kernel, shift),
        "join",
        {"facts": facts, "lines": lines, **basis},
        {
            "x": blocks,
            "factor": struct((held, cap + 16, cap), BF16),
            "inside": block,
            "across": block,
        },
    )
    factor = joined["factor"]
    earlier_factor = lax.ppermute(factor, "seg", onward)
    came = exchange(joined)
    renewed = call(
        grow_kernel,
        "grow",
        {"left": left, "factor": factor},
        {"out": struct(left_env.shape, BF16), "token": token},
        flops=one * 24,
        scratch=[
            pltpu.VMEM((terms, held, cap, cap), BF16),
            pltpu.SemaphoreType.DMA((terms,)),
        ],
        outside=("out",),
    )
    got = made(
        functools.partial(second_kernel, shift),
        "second",
        {
            "v0": joined["x"],
            "left": left,
            "earlier": earlier,
            "factor": earlier_factor,
            "token": renewed["token"],
            **common,
        },
        {"env": struct((terms, held, cap, cap), BF16), **local_outs},
        flops=one * 52,
    )
    basis, lines = relaxed(joined["x"], came, got, got["env"], False)
    done = made(
        functools.partial(finish_kernel, shift),
        "finish",
        {"facts": facts, "lines": lines, **basis},
        {"x": struct(psi.shape, F32), "energy": struct((1,), F32)},
    )
    return (done["x"], done["energy"], renewed["out"])


def solution(mesh):
    return jax.shard_map(
        body,
        mesh=mesh,
        in_specs=(
            P("seg", "sec", None, None),
            P("seg", None, "sec", None, None),
            P("seg", None, "sec", None, None),
            P("seg", None, "sec", None, None),
            P("seg", None, "sec", None, None),
            P("seg", None),
        ),
        out_specs=(P("seg", "sec", None, None), P("seg"), P("seg", None, "sec", None, None)),
        check_vma=False,
    )
```

```python
import functools

import jax
import jax.numpy as jnp
from jax import lax
from jax.experimental import pallas as pl
from jax.experimental.pallas import tpu as pltpu
from jax.sharding import PartitionSpec as P

ITERS = 4
TAU = 0.05
F32 = jnp.float32
BF16 = jnp.bfloat16
LANES = 128
VMEM_LIMIT = 24 << 20
ROWS = 8

VMEM = pl.BlockSpec(memory_space=pltpu.VMEM)
SMEM = pl.BlockSpec(memory_space=pltpu.SMEM)
HBM = pl.BlockSpec(memory_space=pltpu.HBM)


def nn(a, b):
    return lax.dot_general(a, b, (((1,), (0,)), ((), ())), preferred_element_type=F32)


def nt(a, b):
    return lax.dot_general(a, b, (((1,), (1,)), ((), ())), preferred_element_type=F32)


def hop(block, inner, outer):
    return nn(outer, nt(block, inner).astype(BF16))


def masked(block, dim):
    rows = lax.broadcasted_iota(jnp.int32, block.shape, 0)
    cols = lax.broadcasted_iota(jnp.int32, block.shape, 1)
    return jnp.where(jnp.logical_and(rows < dim, cols < dim), block, 0.0)


def local_part(v, env, right, outer, inner, shift, ready=lambda *what: None):
    held = len(v)
    terms = right.shape[1]
    b = [x.astype(BF16) for x in v]
    half = []
    for w in range(terms):
        ready("right", w)
        half.append([nt(b[s], right[0, w, s]).astype(BF16) for s in range(held)])
    image = [None] * held
    ready("hops")
    for s in range(held):
        if s > 0:
            image[s] = hop(b[s - 1], inner[0, 0, s], outer[0, 0, s])
        if s + 1 < held:
            above = hop(b[s + 1], inner[0, 1, s], outer[0, 1, s])
            image[s] = above if image[s] is None else image[s] + above
    for w in range(terms):
        ready("left", w)
        for s in range(held):
            term = nn(env(w, s), half[w][s])
            image[s] = term if image[s] is None else image[s] + term
    return [v[s] * (1.0 + TAU * shift) - TAU * image[s] for s in range(held)]


def dot_rows(basis, last):
    rows = lax.broadcasted_iota(jnp.int32, (ROWS, LANES), 0)
    out = jnp.zeros((ROWS, LANES), F32)
    for i, other in enumerate(basis):
        total = sum(jnp.sum(a * b, axis=0, keepdims=True) for a, b in zip(other, last))
        total = sum(total[:, n : n + LANES] for n in range(0, total.shape[1], LANES))
        out = jnp.where(rows == i, total, out)
    return out


class Facts:
    ODD, FIRST, LIVE, INSIDE, ACROSS, DIM = range(6)

    def __init__(self, ref):
        self.ref = ref

    def row(self, n):
        return self.ref[n : n + 1, 0:1]

    @property
    def odd(self):
        return self.row(self.ODD) == 1

    def dim(self, s):
        return self.row(self.DIM + s)


def swapped(odd, low, high):
    return jnp.where(odd, low, high), jnp.where(odd, high, low)


def start_kernel(
    place, dims_at, psi_at, outer_at, inner_at, v0, inside, across, facts, dims, psi, blocks, arrived
):
    held, cap, _ = psi.shape
    known = pltpu.make_async_copy(dims_at, dims, arrived.at[held + 4])
    known.start()
    copies = [pltpu.make_async_copy(psi_at.at[0, s], psi.at[s], arrived.at[s]) for s in range(held)]
    for n, (side, s) in enumerate(((0, 0), (1, held - 1))):
        for m, array in enumerate((outer_at, inner_at)):
            copies.append(
                pltpu.make_async_copy(
                    array.at[0, side, s], blocks.at[2 * n + m], arrived.at[held + 2 * n + m]
                )
            )
    for copy in copies:
        copy.start()
    known.wait()
    first = place[0] * held
    last = dims.shape[1] - 1
    odd = place[0] % 2
    low_dim = jnp.where(first == 0, 0, dims[0, jnp.maximum(first - 1, 0)])
    high_dim = jnp.where(first + held > last, 0, dims[0, jnp.minimum(first + held, last)])
    live = jnp.int32(0)
    for s in range(dims.shape[1]):
        live = live + dims[0, s] * dims[0, s]
    rows = [
        odd,
        jnp.where(place[1] == 0, 1, 0),
        live,
        jnp.where(odd == 1, low_dim, high_dim),
        jnp.where(odd == 1, high_dim, low_dim),
    ] + [dims[0, first + s] for s in range(held)]
    for n, value in enumerate(rows):
        facts[n : n + 1, :] = jnp.full((1, LANES), value, jnp.int32)
    for copy in copies[:held]:
        copy.wait()
    edges = [masked(psi[s], dims[0, first + s]) for s in range(held)]
    for s in range(held):
        v0[s] = edges[s]
    low = edges[0].astype(BF16)
    high = edges[-1].astype(BF16)
    inside[0] = jnp.where(odd == 1, low, high)
    across[0] = jnp.where(odd == 1, high, low)
    for copy in copies[held:]:
        copy.wait()
    for m in range(2):
        inside[1 + m] = jnp.where(odd == 1, blocks[m], blocks[2 + m])
        across[1 + m] = jnp.where(odd == 1, blocks[2 + m], blocks[m])


def put_local(v, env, r, shift, **ready):
    facts = Facts(r["facts"])
    out = local_part(v, env, r["right"], r["outer"], r["inner"], shift, **ready)
    for s, block in enumerate(out):
        r["q"][s] = block
    if "inside" not in r:
        return
    inside, across = swapped(facts.odd, out[0], out[-1])
    r["inside"][...] = inside.astype(BF16)
    r["across"][...] = across.astype(BF16)


def local_kernel(shift, names, *refs):
    r = dict(zip(names, refs))
    arrived = refs[-1]
    copies = {}
    for n in ("outer", "inner"):
        copies[n] = pltpu.make_async_copy(r[n + "_at"], r[n], arrived.at[len(copies)])
    for n in ("right", "left"):
        for w in range(r[n].shape[1]):
            copies[n, w] = pltpu.make_async_copy(
                r[n + "_at"].at[0, w], r[n].at[0, w], arrived.at[len(copies)]
            )
    order = [("right", w) for w in range(r["right"].shape[1])] + ["outer", "inner"]
    order += [("left", w) for w in range(r["left"].shape[1])]
    for key in order:
        copies[key].start()

    def ready(*what):
        for key in ("outer", "inner") if what == ("hops",) else (what,):
            copies[key].wait()

    v = [r["v0"][s] for s in range(r["v0"].shape[0])]
    put_local(v, lambda w, s: r["left"][0, w, s], r, shift, ready=ready)


def ghosts(k, facts, r):
    came = []
    for n, (name, row) in enumerate((("inside", facts.INSIDE), ("across", facts.ACROSS))):
        ref = r["came_" + name]
        block = (ref[0] if len(ref.shape) == 3 else ref[...]).astype(F32)
        if k > 0:
            block = block - r["given"][n]
        came.append(masked(block, facts.row(row)))
    low, high = swapped(facts.odd, *came)
    return low.astype(BF16), high.astype(BF16)


def put_given(v, facts, r):
    sent = swapped(facts.odd, v[0], v[-1])
    for n, (block, name) in enumerate(zip(sent, ("hops_inside", "hops_across"))):
        r["gives"][n] = TAU * hop(block.astype(BF16), r[name][2], r[name][1])


def step_kernel(k, shift, names, *refs):
    r = dict(zip(names, refs))
    facts = Facts(r["facts"])
    outer, inner = r["outer"], r["inner"]
    held = r["part"].shape[0]
    low, high = ghosts(k, facts, r)
    v = [r["part"][s] for s in range(held)]
    v[0] = v[0] - TAU * hop(low, inner[0, 0, 0], outer[0, 0, 0])
    v[-1] = v[-1] - TAU * hop(high, inner[0, 1, held - 1], outer[0, 1, held - 1])
    v = [masked(block, facts.dim(s)) for s, block in enumerate(v)]
    for s in range(held):
        r["v"][s] = v[s]
    basis = [[r[f"v{i}"][s] for s in range(held)] for i in range(k + 1)]
    if k + 1 < ITERS:
        put_given(basis[k], facts, r)
        left = r["left"]
        env = (lambda w, s: left[0, w, s]) if len(left.shape) == 5 else (lambda w, s: left[w, s])
        put_local(v, env, r, shift)
        if "dots" in r:
            basis = basis + [v]
            for j in range(k + 2):
                r["dots"][j] = dot_rows(basis[: j + 1], basis[j])
    else:
        lanes = lax.broadcasted_iota(jnp.int32, (ROWS, LANES), 1)
        rows = lax.broadcasted_iota(jnp.int32, (ROWS, LANES), 0)
        line = jnp.zeros((1, LANES), F32)
        for j in range(ITERS + 1):
            part = r["dots_before"][j] if j < ITERS else dot_rows(basis + [v], v)
            part = jnp.sum(part, axis=1, keepdims=True)
            line = line + jnp.sum(
                jnp.where(lanes == ROWS * j + rows, part, 0.0), axis=0, keepdims=True
            )
        for n in range(r["line"].shape[0]):
            r["line"][n] = line


def combination(line, live_count, shift):
    lanes = lax.broadcasted_iota(jnp.int32, (1, LANES), 1)
    gram = {}
    for j in range(ITERS + 1):
        for i in range(j + 1):
            gram[i, j] = jnp.sum(
                jnp.where(lanes == ROWS * j + i, line, 0.0), axis=1, keepdims=True
            )
            gram[j, i] = gram[i, j]
    coefs = [jnp.ones((1, 1), F32)]
    energy = None
    for _ in range(ITERS):
        n = len(coefs)
        onto = [sum(coefs[i] * gram[i, j] for i in range(n)) for j in range(n + 1)]
        raised = [sum(coefs[i] * gram[i + 1, j] for i in range(n)) for j in range(1, n + 1)]
        self_dot = sum(coefs[j] * onto[j] for j in range(n))
        cross = sum(coefs[j] * onto[j + 1] for j in range(n))
        square = sum(coefs[j] * raised[j] for j in range(n))
        ratio = cross / self_dot
        gain = 1.0 - ratio
        energy = shift + gain / TAU
        norm = square + gain * (2.0 * cross + gain * self_dot)
        scale = jnp.sqrt(live_count / norm)
        moved = [gain * c for c in coefs] + [jnp.zeros((1, 1), F32)]
        moved = [moved[0]] + [moved[i + 1] + coefs[i] for i in range(n)]
        coefs = [scale * c for c in moved]
    return coefs, energy


def join_kernel(shift, names, *refs):
    r = dict(zip(names, refs))
    facts = Facts(r["facts"])
    line = jnp.sum(r["lines"][...], axis=0)
    coefs, _ = combination(line, facts.row(facts.LIVE).astype(F32), shift)
    held, cap, _ = r["v0"].shape
    pad = r["factor"].shape[1] - cap
    blocks = [sum(c * r[f"v{k}"][s] for k, c in enumerate(coefs)) for s in range(held)]
    for s, block in enumerate(blocks):
        r["x"][s] = block
        r["factor"][s, :cap] = block.astype(BF16)
        dim = jnp.broadcast_to(facts.dim(s).astype(F32), (pad, cap))
        r["factor"][s, cap:] = dim.astype(BF16)
    inside, across = swapped(facts.odd, blocks[0], blocks[-1])
    r["inside"][...] = inside.astype(BF16)
    r["across"][...] = across.astype(BF16)


def grown(env, factor):
    cap = env.shape[0]
    block = factor[:cap]
    product = nn(block.T, nn(env, block).astype(BF16))
    return (product * (1.0 / factor[cap : cap + 1].astype(F32))).astype(BF16)


def grow_kernel(left, factor, out, token, held_out, sent):
    copies = []
    for w in range(left.shape[1]):
        for s in range(left.shape[2]):
            held_out[w, s] = grown(left[0, w, s], factor[s])
        copies.append(pltpu.make_async_copy(held_out.at[w], out.at[0, w], sent.at[w]))
        copies[-1].start()
    token[...] = jnp.zeros_like(token)
    for copy in copies:
        copy.wait()


def second_kernel(shift, names, *refs):
    r = dict(zip(names, refs))
    facts = Facts(r["facts"])
    held = r["v0"].shape[0]
    first = facts.row(facts.FIRST) == 1
    for s in range(held):
        for w in range(r["left"].shape[1]):
            new = grown(r["earlier"][0, w, s], r["factor"][s]).astype(F32)
            kept = r["left"][0, w, s].astype(F32)
            r["env"][w, s] = jnp.where(first, kept, new).astype(BF16)
    v = [r["v0"][s] for s in range(held)]
    put_local(v, lambda w, s: r["env"][w, s], r, shift)


def finish_kernel(shift, names, *refs):
    r = dict(zip(names, refs))
    facts = Facts(r["facts"])
    line = jnp.sum(r["lines"][...], axis=0)
    coefs, energy = combination(line, facts.row(facts.LIVE).astype(F32), shift)
    for s in range(r["v0"].shape[0]):
        r["x"][0, s] = sum(c * r[f"v{k}"][s] for k, c in enumerate(coefs))
    r["energy"][0] = energy[0, 0]


def in_hbm(array):
    return pltpu.with_memory_space_constraint(array, pltpu.HBM)


def struct(shape, dtype):
    return jax.ShapeDtypeStruct(shape, dtype)


def call(kernel, name, ins, outs, flops=0, specs=None, scratch=(), outside=()):
    args = tuple(ins.values())
    values = pl.pallas_call(
        kernel,
        out_shape=tuple(outs.values()),
        in_specs=specs or [VMEM] * len(args),
        out_specs=tuple(
            SMEM if o.shape == (1,) else HBM if n in outside else VMEM for n, o in outs.items()
        ),
        scratch_shapes=scratch,
        name=name,
        compiler_params=pltpu.CompilerParams(vmem_limit_bytes=VMEM_LIMIT),
        cost_estimate=pl.CostEstimate(
            flops=flops,
            transcendentals=0,
            bytes_accessed=sum(a.size * a.dtype.itemsize for a in args),
        ),
    )(*args)
    return dict(zip(outs, values))


def body(psi, left_env, right_env, hop_outer, hop_inner, dims):
    _, terms, held, cap, _ = left_env.shape
    shift = float(terms)
    size = lax.axis_size("sec")
    place = jnp.stack([lax.axis_index("sec"), lax.axis_index("seg")]).astype(jnp.int32)
    block = struct((cap, cap), BF16)
    blocks = struct((held, cap, cap), F32)
    pair = struct((2, cap, cap), F32)
    triple = struct((3, cap, cap), BF16)
    token = struct((ROWS, LANES), F32)
    local_outs = {"q": blocks, "inside": block, "across": block}
    pairs = [(i, i ^ 1) for i in range(size)]
    others = [(i, (i + 1 if i % 2 else i - 1) % size) for i in range(size)]
    segments = lax.axis_size("seg")
    onward = [(i, (i + 1) % segments) for i in range(segments)]
    one = 2 * cap**3

    def exchange(got):
        return {
            "came_across": lax.ppermute(got["across"], "sec", others),
            "came_inside": lax.ppermute(got["inside"], "sec", pairs),
        }

    def made(kernel, name, ins, outs, flops=0, **more):
        names = tuple(ins) + tuple(outs)
        return call(functools.partial(kernel, names), name, ins, outs, flops, **more)

    start = call(
        start_kernel,
        "start",
        {
            "place": place,
            "dims": in_hbm(dims),
            "psi": in_hbm(psi),
            "outer": in_hbm(hop_outer),
            "inner": in_hbm(hop_inner),
        },
        {
            "v0": blocks,
            "inside": triple,
            "across": triple,
            "facts": struct((ROWS * (1 + (4 + held) // ROWS), LANES), jnp.int32),
        },
        specs=[SMEM, HBM, HBM, HBM, HBM],
        scratch=[
            pltpu.SMEM(dims.shape, jnp.int32),
            pltpu.VMEM((held, cap, cap), F32),
            pltpu.VMEM((4, cap, cap), BF16),
            pltpu.SemaphoreType.DMA((held + 5,)),
        ],
    )
    facts = start["facts"]
    came = exchange(start)
    hops = {"hops_inside": came["came_inside"], "hops_across": came["came_across"]}
    earlier = lax.ppermute(left_env, "seg", onward)

    def relaxed(v0, came, got, env):
        basis = {"v0": v0}
        for k in range(ITERS):
            ins = {"part": got["q"], **common, **basis, **came}
            if k > 0:
                ins["given"] = got["gives"]
            if k + 1 < ITERS:
                came = exchange(got)
                ins.update(left=env, **hops)
                outs = {"v": blocks, "gives": pair, **local_outs}
                if k + 2 == ITERS:
                    del outs["inside"], outs["across"]
                    outs["dots"] = struct((ITERS, ROWS, LANES), F32)
            else:
                del ins["right"]
                ins["dots_before"] = got["dots"]
                outs = {"v": blocks, "line": struct((size, 1, LANES), F32)}
            kernel = functools.partial(step_kernel, k, shift)
            got = made(kernel, f"step{k}", ins, outs, flops=one * 36)
            basis[f"v{k + 1}"] = got["v"]
        return basis, lax.all_to_all(got["line"], "sec", 0, 0)

    got = made(
        functools.partial(local_kernel, shift),
        "local",
        {
            "facts": facts,
            "v0": start["v0"],
            "left_at": in_hbm(left_env),
            "right_at": in_hbm(right_env),
            "outer_at": in_hbm(hop_outer),
            "inner_at": in_hbm(hop_inner),
        },
        {
            "left": struct(left_env.shape, BF16),
            "right": struct(right_env.shape, BF16),
            "outer": struct(hop_outer.shape, BF16),
            "inner": struct(hop_inner.shape, BF16),
            **local_outs,
        },
        flops=one * 28,
        specs=[VMEM, VMEM, HBM, HBM, HBM, HBM],
        scratch=[pltpu.SemaphoreType.DMA((2 + 2 * terms,))],
    )
    left = got["left"]
    common = {"facts": facts, **{n: got[n] for n in ("outer", "inner", "right")}}
    basis, lines = relaxed(start["v0"], came, got, left)
    joined = made(
        functools.partial(join_kernel, shift),
        "join",
        {"facts": facts, "lines": lines, **basis},
        {
            "x": blocks,
            "factor": struct((held, cap + 16, cap), BF16),
            "inside": block,
            "across": block,
        },
    )
    factor = joined["factor"]
    earlier_factor = lax.ppermute(factor, "seg", onward)
    came = exchange(joined)
    renewed = call(
        grow_kernel,
        "grow",
        {"left": left, "factor": factor},
        {"out": struct(left_env.shape, BF16), "token": token},
        flops=one * 24,
        scratch=[
            pltpu.VMEM((terms, held, cap, cap), BF16),
            pltpu.SemaphoreType.DMA((terms,)),
        ],
        outside=("out",),
    )
    got = made(
        functools.partial(second_kernel, shift),
        "second",
        {
            "v0": joined["x"],
            "left": left,
            "earlier": earlier,
            "factor": earlier_factor,
            "token": renewed["token"],
            **common,
        },
        {"env": struct((terms, held, cap, cap), BF16), **local_outs},
        flops=one * 52,
    )
    basis, lines = relaxed(joined["x"], came, got, got["env"])
    done = made(
        functools.partial(finish_kernel, shift),
        "finish",
        {"facts": facts, "lines": lines, **basis},
        {"x": struct(psi.shape, F32), "energy": struct((1,), F32)},
    )
    return (done["x"], done["energy"], renewed["out"])


def solution(mesh):
    return jax.shard_map(
        body,
        mesh=mesh,
        in_specs=(
            P("seg", "sec", None, None),
            P("seg", None, "sec", None, None),
            P("seg", None, "sec", None, None),
            P("seg", None, "sec", None, None),
            P("seg", None, "sec", None, None),
            P("seg", None),
        ),
        out_specs=(P("seg", "sec", None, None), P("seg"), P("seg", None, "sec", None, None)),
        check_vma=False,
    )
```
